32 devices in a mesh: grp: 8 (over y, x, core), blk: 4 (over z).
Axes of the slice: x: 2, y: 2, z: 4, core: 2. Of those that a mesh axis runs over, the one named last changes fastest.
Arguments:
- image_tokens: bfloat16 [3, 7168, 2432], P(None, ('grp', 'blk')), may hold values from -128 to 128, as said below
- text_tokens: bfloat16 [3, 512, 2432], P(None, ('grp', 'blk')), may hold values from -128 to 128, as said below
- lengths: int32 [8], P('grp'), may hold values from 224 to 896
- image_weight: bfloat16 [2432, 2432], P('grp'), may hold values from -0.125 to 0.125
- text_weight: bfloat16 [2432, 2432], P('grp'), may hold values from -0.125 to 0.125
- gate_values: float32 [8, 2, 2432], P('grp'), may hold values from 0.5 to 2
Outputs:
- image_update: bfloat16 [7168, 2432], P(('grp', 'blk'))
- text_update: bfloat16 [512, 2432], P(('grp', 'blk'))
The draws below stay inside these ranges and needn't reach their ends.
Inputs may be any that keep to these rules, and one draw needn't show every extreme that they name: `image_tokens`: Real-valued queries, keys and values. `text_tokens`: Real-valued queries, keys and values. Request g has lengths[g] image tokens; its slots from that index up to 896 are padding, never valid keys.
All inputs are finite; a program needn't handle non-finite values.
Results may differ from the reference program's by a relative error of at most 0.0085.
Values may be sent and summed in bfloat16 or wider, within the bound.
A program may use at most 256 MiB of HBM per device.

```python
import jax
import jax.numpy as jnp
from jax import lax

HEADS = 38
HEAD_DIM = 64
D = 2432
TOK_DEV = 224
TOK_GRP = 896
GROUPS = 8
IMG = 7168
TXT = 512


def base_values(key, row_count):
    first_key = jax.random.fold_in(key, 0)
    factors = jnp.array([2.0, 1.0, 2.0], jnp.float32).reshape(3, 1, 1)
    raw = jnp.clip(jax.random.normal(first_key, (3, row_count, D), jnp.float32), -4.0, 4.0)
    return raw * factors


def draw_image_tokens(key, part):
    values = base_values(jax.random.fold_in(key, 11), IMG)
    return values.astype(jnp.bfloat16)


def draw_text_tokens(key, part):
    values = base_values(jax.random.fold_in(key, 21), TXT)
    return values.astype(jnp.bfloat16)


def place_ends(drawn, stream_key, low, largest):
    index_at = [jax.random.randint(jax.random.fold_in(stream_key, axis), (), 0, length) for axis, length in enumerate(drawn.shape)]
    main_axis = drawn.shape.index(max(drawn.shape))
    next_to = index_at[:main_axis] + [(index_at[main_axis] + 1) % drawn.shape[main_axis]] + index_at[main_axis + 1:]
    return drawn.at[tuple(index_at)].set(low).at[tuple(next_to)].set(largest)


def shard_levels(own_key, shape, cuts, least, high):
    factor_of, own = 1.0, jax.random.fold_in(own_key, 6)
    for axis_at, shards_of in cuts:
        steps = jnp.exp(jax.random.uniform(jax.random.fold_in(own, axis_at), (shards_of,), jnp.float32, least / len(cuts), high / len(cuts)))
        factor_of = factor_of * jnp.repeat(steps, shape[axis_at] // shards_of).reshape([-1 if axis == axis_at else 1 for axis in range(len(shape))])
    return factor_of


def noise(key, extent, spread, limit, cuts=(), kind=jnp.bfloat16):
    result = spread * jax.random.normal(key, extent, jnp.float32)
    if cuts:
        result = result * shard_levels(key, extent, cuts, -0.22, 0.18)
    return jnp.clip(result, -limit, limit).astype(kind)


def setup_inputs(seed: int = 0) -> dict:
    streams_of = jax.random.split(jax.random.key(seed), 7)
    image_tokens = draw_image_tokens(jax.random.fold_in(streams_of[6], 71), 0)
    text_tokens = draw_text_tokens(jax.random.fold_in(streams_of[6], 71), 0)
    lengths = place_ends(jax.random.randint(streams_of[2], (GROUPS,), TOK_DEV, TOK_GRP + 1), jax.random.fold_in(streams_of[2], 1), TOK_DEV, TOK_GRP).astype(jnp.int32)
    image_weight = noise(streams_of[3], (D, D), D ** -0.5, 0.125, ((0, 8),))
    text_weight = noise(streams_of[4], (D, D), D ** -0.5, 0.125, ((0, 8),))
    gate_values = jnp.clip(0.5 + 1.5 * jax.random.uniform(streams_of[5], (GROUPS, 2, D), jnp.float32) ** shard_levels(streams_of[5], (GROUPS, 2, D), ((0, 8),), -0.2, 0.2), 0.5, 2.0)
    return {"image_tokens": image_tokens, "text_tokens": text_tokens, "lengths": lengths, "image_weight": image_weight, "text_weight": text_weight, "gate_values": gate_values}


NEG_FILL = -1.0e30


def attend(queries, key_rows, value_rows, usable):
    query_count = queries.shape[0]
    key_count = key_rows.shape[0]
    query_heads = jnp.transpose(queries.reshape(query_count, HEADS, HEAD_DIM), (1, 0, 2))
    key_heads = jnp.transpose(key_rows.reshape(key_count, HEADS, HEAD_DIM), (1, 0, 2))
    value_heads = jnp.transpose(value_rows.reshape(key_count, HEADS, HEAD_DIM), (1, 0, 2))

    def one_head(inputs):
        query_head, key_head, value_head = inputs
        scores = jnp.dot(query_head, key_head.T, preferred_element_type=jnp.float32) * (HEAD_DIM ** -0.5)
        scores = jnp.where(usable[None, :], scores, NEG_FILL)
        row_max = jnp.max(scores, axis=1, keepdims=True)
        probs = jnp.where(usable[None, :], jnp.exp(scores - row_max), 0.0)
        totals = jnp.sum(probs, axis=1, keepdims=True)
        summed = jnp.dot(probs.astype(jnp.bfloat16), value_head, preferred_element_type=jnp.float32)
        return summed / totals

    outputs = lax.map(one_head, (query_heads, key_heads, value_heads))
    merged = jnp.transpose(outputs, (1, 0, 2)).reshape(query_count, HEADS * HEAD_DIM)
    return merged.astype(jnp.bfloat16)


def reference(image_tokens, text_tokens, lengths, image_weight, text_weight, gate_values):
    group_count = lengths.shape[0]
    model_width = image_tokens.shape[2]
    image_rows = image_tokens.shape[1] // group_count
    text_rows = text_tokens.shape[1] // group_count
    image_groups = jnp.transpose(image_tokens.reshape(3, group_count, image_rows, model_width), (1, 0, 2, 3))
    text_groups = jnp.transpose(text_tokens.reshape(3, group_count, text_rows, model_width), (1, 0, 2, 3))

    def one_group(inputs):
        image_part, text_part, length, gates = inputs
        queries = jnp.concatenate([image_part[0], text_part[0]], axis=0)
        key_rows = jnp.concatenate([image_part[1], text_part[1]], axis=0)
        value_rows = jnp.concatenate([image_part[2], text_part[2]], axis=0)
        usable = jnp.concatenate([jnp.arange(image_rows, dtype=jnp.int32) < length,
                                  jnp.ones((text_rows,), dtype=jnp.bool_)], axis=0)
        attended = attend(queries, key_rows, value_rows, usable)
        image_out = jnp.dot(attended[:image_rows], image_weight, preferred_element_type=jnp.float32) * gates[0]
        text_out = jnp.dot(attended[image_rows:], text_weight, preferred_element_type=jnp.float32) * gates[1]
        return image_out.astype(jnp.bfloat16), text_out.astype(jnp.bfloat16)

    image_out, text_out = lax.map(one_group, (image_groups, text_groups, lengths, gate_values))
    return image_out.reshape(-1, model_width), text_out.reshape(-1, model_width)
```

```python
import functools

import jax
import jax.numpy as jnp
from jax import lax
from jax.experimental import pallas as pl
from jax.experimental.pallas import tpu as pltpu
from jax.sharding import PartitionSpec as P

HEADS = 38
LANES = 128
MESH = pl.DeviceIdType.MESH


def remote(src, dst, send, recv, axis, peer):
    return pltpu.make_async_remote_copy(
        src_ref=src, dst_ref=dst, send_sem=send, recv_sem=recv,
        device_id={axis: peer}, device_id_type=MESH)


def row_parts(rows, parts, unit):
    base, extra = divmod(rows // unit, parts)
    sizes = [(base + (1 if j < extra else 0)) * unit for j in range(parts)]
    return [(sum(sizes[:j]), sizes[j]) for j in range(parts) if sizes[j]]


def column_tiles(width, tile):
    return [(at, min(tile, width - at)) for at in range(0, width, tile)]


class WeightGather:
    def __init__(self, group_count, shard, full, local, send, recv, sib_send, sib_recv):
        self.shard, self.full, self.local = shard, full, local
        self.send, self.recv, self.sib_send, self.sib_recv = send, recv, sib_send, sib_recv
        self.rows = shard.shape[0]
        self.unit = 16 if self.rows % 16 == 0 else 8
        self.bits = group_count.bit_length() - 1
        self.far = list(range(1, self.bits))
        self.parts = row_parts(self.rows, max(1, len(self.far)), self.unit)
        self.me = lax.axis_index("grp")

    def flip(self, mask):
        at = self.me
        for k in range(self.bits):
            if mask >> k & 1:
                at = at + (1 - 2 * ((self.me // (1 << k)) % 2)) * (1 << k)
        return at

    def order(self, j):
        return self.far[j:] + self.far[:j] if self.far else []

    def masks(self, level):
        return [m for m in range(0, 1 << self.bits, 2) if bin(m).count("1") == level]

    def piece(self, j, mask):
        first, size = self.parts[j]
        return self.full.at[pl.ds(pl.multiple_of(self.flip(mask) * self.rows + first, self.unit), size), :]

    def source(self, j, mask):
        first, size = self.parts[j]
        return self.shard.at[pl.ds(first, size), :] if mask == 0 else self.piece(j, mask)

    def far_copies(self, j, mask):
        order = self.order(j)
        done = max([order.index(k) for k in order if mask >> k & 1], default=-1)
        return [
            remote(self.source(j, mask), self.piece(j, mask), self.send.at[j, (mask | 1 << k) // 2],
                   self.recv.at[j, (mask | 1 << k) // 2], "grp", self.flip(1 << k))
            for k in order[done + 1:]
        ]

    def far_arrival(self, j, mask):
        return remote(self.piece(j, mask), self.piece(j, mask), self.send.at[j, mask // 2],
                      self.recv.at[j, mask // 2], "grp", self.me)

    def near_copy(self, j, mask):
        return remote(self.source(j, mask), self.piece(j, mask), self.sib_send.at[j, mask // 2],
                      self.sib_recv.at[j, mask // 2], "grp", self.flip(1))

    def near_arrival(self, j, mask):
        return remote(self.piece(j, mask | 1), self.piece(j, mask | 1), self.sib_send.at[j, mask // 2],
                      self.sib_recv.at[j, mask // 2], "grp", self.me)

    def own(self):
        return pltpu.make_async_copy(
            self.shard, self.full.at[pl.ds(pl.multiple_of(self.me * self.rows, self.unit), self.rows), :], self.local)

    def advance(self, level):
        if level > len(self.far):
            return
        for mask in self.masks(level):
            for j in range(len(self.parts)):
                if level:
                    self.far_arrival(j, mask).wait_recv()
                for copy in self.far_copies(j, mask):
                    copy.start()
                if self.bits:
                    self.near_copy(j, mask).start()
        if level == 0:
            self.own().start()

    def finish(self):
        self.own().wait()
        for level in range(len(self.far) + 1):
            for mask in self.masks(level):
                for j in range(len(self.parts)):
                    if self.bits:
                        self.near_arrival(j, mask).wait_recv()

    def drain(self):
        for level in range(len(self.far) + 1):
            for mask in self.masks(level):
                for j in range(len(self.parts)):
                    for copy in self.far_copies(j, mask):
                        copy.wait_send()
                    if self.bits:
                        self.near_copy(j, mask).wait_send()


def block_kernel(
    n, group_count, head_size,
    length, img, txt, image_shard, text_shard, gates, out_img, out_txt,
    qkv, shared_kv, shared_q, attended, done, keys, first_values, second_values, valid, image_full, text_full,
    image_acc, text_acc,
    in_send, in_recv, in_local, out_send, out_recv, out_local, kv_send, kv_recv, shared_local,
    w_local, w_send, w_recv, w_sib_send, w_sib_recv,
):
    me = lax.axis_index("blk")
    image_rows, text_rows, width = img.shape[1], txt.shape[1], img.shape[2]
    span = image_rows + text_rows
    pairs = width // LANES
    base, extra = divmod(pairs, n)
    streams = ((img, 0, image_rows), (txt, image_rows, text_rows))

    weights = [
        WeightGather(group_count, shard, full, w_local.at[i], w_send.at[i], w_recv.at[i], w_sib_send.at[i], w_sib_recv.at[i])
        for i, (shard, full) in enumerate(((image_shard, image_full), (text_shard, text_full)))
    ]

    barrier = pltpu.get_barrier_semaphore()
    for d in range(1, n):
        pl.semaphore_signal(barrier, inc=1, device_id={"blk": lax.rem(me + d, n)}, device_id_type=MESH)
    for k in range(weights[0].bits):
        pl.semaphore_signal(barrier, inc=1, device_id={"grp": weights[0].flip(1 << k)}, device_id_type=MESH)
    pl.semaphore_wait(barrier, n - 1 + weights[0].bits)

    def columns(b, p):
        return pl.ds(pl.multiple_of((b * base + p) * LANES, LANES), LANES)

    def rows_of(b, first, count):
        return pl.ds(pl.multiple_of(b * span + first, 16), count)

    def in_copies(p, dest, owner, d):
        return [
            remote(src.at[:, :, columns(dest, p)], qkv.at[p, :, rows_of(owner, first, count), :],
                   in_send.at[p, d, i], in_recv.at[p, owner, i], "blk", dest)
            for i, (src, first, count) in enumerate(streams)
        ]

    def own_copies(p):
        return [
            pltpu.make_async_copy(
                src.at[:, :, columns(me, p)], qkv.at[p, :, rows_of(me, first, count), :], in_local.at[p, i])
            for i, (src, first, count) in enumerate(streams)
        ]

    def out_copy(p, dest, owner, d):
        return remote(done.at[p, dest], attended.at[owner * base + p],
                      out_send.at[p, d], out_recv.at[p, owner], "blk", dest)

    def own_out(p):
        return pltpu.make_async_copy(done.at[p, me], attended.at[me * base + p], out_local.at[p])

    shared_cols = pl.ds(n * base * LANES, extra * LANES)

    def kv_direct(owner, dest, side):
        return [
            remote(src.at[pl.ds(1, 2), :, shared_cols], shared_kv.at[:, rows_of(owner, first, count), :],
                   kv_send.at[side, 0, i], kv_recv.at[owner, i], "blk", dest)
            for i, (src, first, count) in enumerate(streams)
        ]

    def kv_onward(owner, dest, side, hop):
        block = shared_kv.at[:, rows_of(owner, 0, span), :]
        return remote(block, block, kv_send.at[side, hop, 0], kv_recv.at[owner, 0], "blk", dest)

    def shared_own():
        copies = []
        for i, (src, first, count) in enumerate(streams):
            copies.append(pltpu.make_async_copy(
                src.at[pl.ds(1, 2), :, shared_cols], shared_kv.at[:, rows_of(me, first, count), :], shared_local.at[0, i]))
            copies.append(pltpu.make_async_copy(
                src.at[0, :, shared_cols], shared_q.at[pl.ds(first, count), :], shared_local.at[1, i]))
        return copies

    def neighbour(side):
        return (me + 1, me + 1 < n) if side == 0 else (me - 1, me >= 1)

    def source(side, hop):
        return (me - hop, me >= hop) if side == 0 else (me + hop, me + hop < n)

    def start_shared():
        for side in range(2):
            dest, there = neighbour(side)

            @pl.when(there)
            def _():
                for copy in kv_direct(me, dest, side):
                    copy.start()
        for copy in shared_own():
            copy.start()

    def advance_shared(hop):
        for side in range(2):
            owner, known = source(side, hop)
            dest, there = neighbour(side)

            @pl.when(known)
            def _():
                if hop == 1:
                    for copy in kv_direct(owner, me, side):
                        copy.wait_recv()
                else:
                    kv_onward(owner, me, side, hop - 1).wait_recv()

            if hop < n - 1:
                @pl.when(known & there)
                def _():
                    kv_onward(owner, dest, side, hop).start()

    def drain_shared():
        for side in range(2):
            dest, there = neighbour(side)

            @pl.when(there)
            def _():
                for copy in kv_direct(me, dest, side):
                    copy.wait_send()
            for hop in range(1, n - 1):
                owner, known = source(side, hop)

                @pl.when(known & there)
                def _():
                    kv_onward(owner, dest, side, hop).wait_send()

    order = sorted(range(1, n), key=lambda d: abs(d - n / 2))

    def send_in(p):
        for d in order:
            for copy in in_copies(p, lax.rem(me + d, n), me, d):
                copy.start()
        for copy in own_copies(p):
            copy.start()

    first_half = lax.broadcasted_iota(jnp.int32, (span, LANES), 1) < head_size

    def prepare(block_keys, block_values):
        half = lax.broadcasted_iota(jnp.int32, (n * span, LANES), 1) < head_size
        ones = jnp.ones((n * span, LANES), jnp.bfloat16)
        usable = valid[...]
        k = block_keys()
        keys[...] = jnp.where(usable > 0.5, k, jnp.broadcast_to(k[0:1], k.shape))
        v = block_values()
        first_values[...] = jnp.where(half, v, ones) * usable
        second_values[...] = jnp.where(half, ones, v) * usable

    def attend_rows(queries):
        queries = queries * jnp.asarray(head_size ** (-0.5), jnp.bfloat16)
        zeros = jnp.zeros_like(queries)
        parts = []
        for own, values in ((jnp.where(first_half, queries, zeros), first_values),
                            (jnp.where(first_half, zeros, queries), second_values)):
            scores = lax.dot_general(own, keys[...], (((1,), (1,)), ((), ())), preferred_element_type=jnp.float32)
            probs = jnp.exp(scores - jnp.max(scores, axis=1, keepdims=True)).astype(jnp.bfloat16)
            parts.append(jnp.dot(probs, values[...], preferred_element_type=jnp.float32))
        summed = jnp.where(first_half, parts[0], parts[1])
        totals = pltpu.roll(jnp.where(first_half, parts[1], parts[0]), head_size, axis=1)
        return (summed / totals).astype(jnp.bfloat16)

    def attend_pair(p):
        for copy in own_copies(p):
            copy.wait()
        for d in range(1, n):
            for copy in in_copies(p, me, lax.rem(me + d, n), d):
                copy.wait_recv()
        if p + 2 < base:
            send_in(p + 2)
        prepare(lambda: qkv[p, 1], lambda: qkv[p, 2])

        def one_block(j, _):
            dest = lax.rem(me + n // 2 + j, n)
            done[p, dest] = attend_rows(qkv[p, 0, rows_of(dest, 0, span), :])

            @pl.when(dest != me)
            def _():
                out_copy(p, dest, me, lax.rem(dest - me + n, n)).start()

            return 0

        lax.fori_loop(0, n, one_block, 0)
        own_out(p).start()

    def attend_shared():
        for copy in shared_own():
            copy.wait()
        for e in range(extra):
            cols = pl.ds(e * LANES, LANES)
            prepare(lambda: shared_kv[0, :, cols], lambda: shared_kv[1, :, cols])
            attended[n * base + e] = attend_rows(shared_q[:, cols])

    def project(acc, full, rows, chosen, start, finish):
        left = jnp.concatenate([attended[c, rows, :] for c in chosen], axis=1)
        for at, size in column_tiles(width, 256):
            right = jnp.concatenate([full[pl.ds(c * LANES, LANES), pl.ds(at, size)] for c in chosen], axis=0)
            part = jnp.dot(left, right, preferred_element_type=jnp.float32)
            if not start:
                part = part + acc[:, pl.ds(at, size)]
            if finish is None:
                acc[:, pl.ds(at, size)] = part
            else:
                out, gate = finish
                out[:, pl.ds(at, size)] = (part * gates[0, pl.ds(gate, 1), pl.ds(at, size)]).astype(jnp.bfloat16)

    text_span = pl.ds(image_rows, text_rows)
    image_span = pl.ds(0, image_rows)

    if extra:
        start_shared()
    for p in range(min(2, base)):
        send_in(p)
    weights[0].advance(0)

    for b in range(n):
        at = lax.broadcasted_iota(jnp.int32, (span, LANES), 0)
        usable = (at >= image_rows) | (b * image_rows + at < length[0])
        valid[pl.ds(b * span, span), :] = jnp.where(usable, 1.0, 0.0).astype(jnp.bfloat16)

    if extra:
        for hop in range(1, n):
            advance_shared(hop)
    weights[0].advance(1)
    weights[1].advance(0)
    for p in range(base):
        attend_pair(p)
        if p == 0:
            for level in range(2, len(weights[0].far) + 1):
                weights[0].advance(level)
            if extra:
                attend_shared()
        if p == base - 2 or base == 1:
            weights[1].advance(1)
    weights[0].finish()
    started = bool(extra)
    if extra:
        project(image_acc, image_full, image_span, [n * base + e for e in range(extra)], True, None)
    for p in range(base):
        own_out(p).wait()
        for d in range(1, n):
            out_copy(p, me, lax.rem(me + d, n), d).wait_recv()
        chosen = [b * base + p for b in range(n)]
        last = p == base - 1
        if last:
            for level in range(2, len(weights[1].far) + 1):
                weights[1].advance(level)
            weights[1].finish()
            if extra:
                project(text_acc, text_full, text_span, [n * base + e for e in range(extra)], True, None)
            for q in range(base - 1):
                project(text_acc, text_full, text_span, [b * base + q for b in range(n)], not extra and q == 0, None)
            project(text_acc, text_full, text_span, chosen, not extra and base == 1, (out_txt, 1))
        project(image_acc, image_full, image_span, chosen, not started, (out_img, 0) if last else None)
        started = True

    for p in range(base):
        for d in range(1, n):
            peer = lax.rem(me + d, n)
            for copy in in_copies(p, peer, me, d):
                copy.wait_send()
            out_copy(p, peer, me, d).wait_send()
    if extra:
        drain_shared()
    for weight in weights:
        weight.drain()


def per_device(image_tokens, text_tokens, lengths, image_weight, text_weight, gate_values):
    image_rows, text_rows, width = image_tokens.shape[1], text_tokens.shape[1], image_tokens.shape[2]
    n, group_count = lax.axis_size("blk"), lax.axis_size("grp")
    span = image_rows + text_rows
    pairs = width // LANES
    base, extra = divmod(pairs, n)
    bits = group_count.bit_length() - 1
    parts, masks = max(1, bits - 1), max(1, group_count // 2)
    dma = pltpu.SemaphoreType.DMA
    bf16, f32 = jnp.bfloat16, jnp.float32
    any_space = pl.BlockSpec(memory_space=pl.ANY)
    vmem = pl.BlockSpec(memory_space=pltpu.VMEM)
    wide = max(1, extra) * LANES
    return pl.pallas_call(
        functools.partial(block_kernel, n, group_count, width // HEADS),
        out_shape=(
            jax.ShapeDtypeStruct((image_rows, width), bf16),
            jax.ShapeDtypeStruct((text_rows, width), bf16),
        ),
        in_specs=[pl.BlockSpec(memory_space=pltpu.SMEM), any_space, any_space, any_space, any_space, vmem],
        out_specs=(vmem, vmem),
        scratch_shapes=[
            pltpu.VMEM((base, 3, n * span, LANES), bf16),
            pltpu.VMEM((2, n * span, wide), bf16),
            pltpu.VMEM((span, wide), bf16),
            pltpu.VMEM((pairs, span, LANES), bf16),
            pltpu.VMEM((base, n, span, LANES), bf16),
            pltpu.VMEM((n * span, LANES), bf16),
            pltpu.VMEM((n * span, LANES), bf16),
            pltpu.VMEM((n * span, LANES), bf16),
            pltpu.VMEM((n * span, LANES), bf16),
            pltpu.VMEM((width, width), bf16),
            pltpu.VMEM((width, width), bf16),
            pltpu.VMEM((image_rows, width), f32),
            pltpu.VMEM((text_rows, width), f32),
            dma((base, n, 2)), dma((base, n, 2)), dma((base, 2)),
            dma((base, n)), dma((base, n)), dma((base,)),
            dma((2, n, 2)), dma((n, 2)), dma((2, 2)),
            dma((2,)), dma((2, parts, masks)), dma((2, parts, masks)), dma((2, parts, masks)), dma((2, parts, masks)),
        ],
        compiler_params=pltpu.CompilerParams(
            collective_id=0, has_side_effects=True, vmem_limit_bytes=56 * 1024 * 1024
        ),
        name="attend",
    )(lengths, image_tokens, text_tokens, image_weight, text_weight, gate_values)


def solution(mesh):
    in_specs = (
        P(None, ("grp", "blk"), None),
        P(None, ("grp", "blk"), None),
        P("grp"),
        P("grp", None),
        P("grp", None),
        P("grp", None, None),
    )
    out_specs = (P(("grp", "blk"), None), P(("grp", "blk"), None))
    return jax.shard_map(
        per_device, mesh=mesh, in_specs=in_specs, out_specs=out_specs, check_vma=False
    )
```

```python
import functools

import jax
import jax.numpy as jnp
from jax import lax
from jax.experimental import pallas as pl
from jax.experimental.pallas import tpu as pltpu
from jax.sharding import PartitionSpec as P

HEADS = 38
LANES = 128
MESH = pl.DeviceIdType.MESH


def remote(src, dst, send, recv, axis, peer):
    return pltpu.make_async_remote_copy(
        src_ref=src, dst_ref=dst, send_sem=send, recv_sem=recv,
        device_id={axis: peer}, device_id_type=MESH)


def row_parts(rows, parts, unit):
    base, extra = divmod(rows // unit, parts)
    sizes = [(base + (1 if j < extra else 0)) * unit for j in range(parts)]
    return [(sum(sizes[:j]), sizes[j]) for j in range(parts) if sizes[j]]


def column_tiles(width, tile):
    return [(at, min(tile, width - at)) for at in range(0, width, tile)]


class WeightGather:
    def __init__(self, group_count, shard, full, local, send, recv, sib_send, sib_recv):
        self.shard, self.full, self.local = shard, full, local
        self.send, self.recv, self.sib_send, self.sib_recv = send, recv, sib_send, sib_recv
        self.rows = shard.shape[0]
        self.unit = 16 if self.rows % 16 == 0 else 8
        self.bits = group_count.bit_length() - 1
        self.far = list(range(1, self.bits))
        self.parts = row_parts(self.rows, max(1, len(self.far)), self.unit)
        self.me = lax.axis_index("grp")

    def flip(self, mask):
        at = self.me
        for k in range(self.bits):
            if mask >> k & 1:
                at = at + (1 - 2 * ((self.me // (1 << k)) % 2)) * (1 << k)
        return at

    def order(self, j):
        return self.far[j:] + self.far[:j] if self.far else []

    def masks(self, level):
        return [m for m in range(0, 1 << self.bits, 2) if bin(m).count("1") == level]

    def piece(self, j, mask):
        first, size = self.parts[j]
        return self.full.at[pl.ds(pl.multiple_of(self.flip(mask) * self.rows + first, self.unit), size), :]

    def source(self, j, mask):
        first, size = self.parts[j]
        return self.shard.at[pl.ds(first, size), :] if mask == 0 else self.piece(j, mask)

    def far_copies(self, j, mask):
        order = self.order(j)
        done = max([order.index(k) for k in order if mask >> k & 1], default=-1)
        return [
            remote(self.source(j, mask), self.piece(j, mask), self.send.at[j, (mask | 1 << k) // 2],
                   self.recv.at[j, (mask | 1 << k) // 2], "grp", self.flip(1 << k))
            for k in order[done + 1:]
        ]

    def far_arrival(self, j, mask):
        return remote(self.piece(j, mask), self.piece(j, mask), self.send.at[j, mask // 2],
                      self.recv.at[j, mask // 2], "grp", self.me)

    def near_copy(self, j, mask):
        return remote(self.source(j, mask), self.piece(j, mask), self.sib_send.at[j, mask // 2],
                      self.sib_recv.at[j, mask // 2], "grp", self.flip(1))

    def near_arrival(self, j, mask):
        return remote(self.piece(j, mask | 1), self.piece(j, mask | 1), self.sib_send.at[j, mask // 2],
                      self.sib_recv.at[j, mask // 2], "grp", self.me)

    def own(self):
        return pltpu.make_async_copy(
            self.shard, self.full.at[pl.ds(pl.multiple_of(self.me * self.rows, self.unit), self.rows), :], self.local)

    def advance(self, level):
        if level > len(self.far):
            return
        for mask in self.masks(level):
            for j in range(len(self.parts)):
                if level:
                    self.far_arrival(j, mask).wait_recv()
                for copy in self.far_copies(j, mask):
                    copy.start()
                if self.bits:
                    self.near_copy(j, mask).start()
        if level == 0:
            self.own().start()

    def finish(self):
        self.own().wait()
        for level in range(len(self.far) + 1):
            for mask in self.masks(level):
                for j in range(len(self.parts)):
                    if self.bits:
                        self.near_arrival(j, mask).wait_recv()

    def drain(self):
        for level in range(len(self.far) + 1):
            for mask in self.masks(level):
                for j in range(len(self.parts)):
                    for copy in self.far_copies(j, mask):
                        copy.wait_send()
                    if self.bits:
                        self.near_copy(j, mask).wait_send()


def block_kernel(
    n, group_count, head_size,
    length_in, img, txt, image_shard, text_shard, gates_in, out_img, out_txt,
    length, gates,
    qkv, shared_kv, shared_q, attended, done, keys, first_values, second_values, valid, image_full, text_full,
    image_acc, text_acc,
    in_send, in_recv, in_local, out_send, out_recv, out_local, kv_send, kv_pass, kv_recv, shared_local,
    w_local, w_send, w_recv, w_sib_send, w_sib_recv, small_local,
):
    me = lax.axis_index("blk")
    image_rows, text_rows, width = img.shape[1], txt.shape[1], img.shape[2]
    span = image_rows + text_rows
    pairs = width // LANES
    base, extra = divmod(pairs, n)
    streams = ((img, 0, image_rows), (txt, image_rows, text_rows))

    weights = [
        WeightGather(group_count, shard, full, w_local.at[i], w_send.at[i], w_recv.at[i], w_sib_send.at[i], w_sib_recv.at[i])
        for i, (shard, full) in enumerate(((image_shard, image_full), (text_shard, text_full)))
    ]

    length_copy = pltpu.make_async_copy(length_in, length, small_local.at[0])
    gates_copy = pltpu.make_async_copy(gates_in, gates, small_local.at[1])
    length_copy.start()
    gates_copy.start()

    barrier = pltpu.get_barrier_semaphore()
    for d in range(1, n):
        pl.semaphore_signal(barrier, inc=1, device_id={"blk": lax.rem(me + d, n)}, device_id_type=MESH)
    for k in range(weights[0].bits):
        pl.semaphore_signal(barrier, inc=1, device_id={"grp": weights[0].flip(1 << k)}, device_id_type=MESH)
    pl.semaphore_wait(barrier, n - 1 + weights[0].bits)

    def columns(b, p):
        return pl.ds(pl.multiple_of((b * base + p) * LANES, LANES), LANES)

    def rows_of(b, first, count):
        return pl.ds(pl.multiple_of(b * span + first, 16), count)

    def in_copies(p, dest, owner, d):
        return [
            remote(src.at[:, :, columns(dest, p)], qkv.at[p, :, rows_of(owner, first, count), :],
                   in_send.at[p, d, i], in_recv.at[p, owner, i], "blk", dest)
            for i, (src, first, count) in enumerate(streams)
        ]

    def own_copies(p):
        return [
            pltpu.make_async_copy(
                src.at[:, :, columns(me, p)], qkv.at[p, :, rows_of(me, first, count), :], in_local.at[p, i])
            for i, (src, first, count) in enumerate(streams)
        ]

    def out_copy(p, dest, owner, d):
        return remote(done.at[p, dest], attended.at[owner * base + p],
                      out_send.at[p, d], out_recv.at[p, owner], "blk", dest)

    def own_out(p):
        return pltpu.make_async_copy(done.at[p, me], attended.at[me * base + p], out_local.at[p])

    shared_cols = pl.ds(n * base * LANES, extra * LANES)

    middle = n // 2
    halves = (range(middle), range(middle, n))
    doors = (middle - 1, middle)

    def kv_direct(owner, dest):
        return [
            remote(src.at[pl.ds(1, 2), :, shared_cols], shared_kv.at[:, rows_of(owner, first, count), :],
                   kv_send.at[dest, i], kv_recv.at[owner, i], "blk", dest)
            for i, (src, first, count) in enumerate(streams)
        ]

    def kv_onward(owner, dest):
        block = shared_kv.at[:, rows_of(owner, 0, span), :]
        return remote(block, block, kv_pass.at[owner, dest], kv_recv.at[owner, 0], "blk", dest)

    def shared_own():
        copies = []
        for i, (src, first, count) in enumerate(streams):
            copies.append(pltpu.make_async_copy(
                src.at[pl.ds(1, 2), :, shared_cols], shared_kv.at[:, rows_of(me, first, count), :], shared_local.at[0, i]))
            copies.append(pltpu.make_async_copy(
                src.at[0, :, shared_cols], shared_q.at[pl.ds(first, count), :], shared_local.at[1, i]))
        return copies

    def each_half(act):
        for side in range(2):
            if len(halves[side]):
                @pl.when((me < middle) if side == 0 else (me >= middle))
                def _():
                    act(side)

    def start_shared():
        def act(side):
            if len(halves[1 - side]):
                for copy in kv_direct(me, doors[1 - side]):
                    copy.start()
            for dest in halves[side]:
                @pl.when(dest != me)
                def _():
                    for copy in kv_direct(me, dest):
                        copy.start()

        each_half(act)
        for copy in shared_own():
            copy.start()

    def pass_shared():
        def act(side):
            door = doors[side]

            @pl.when(me == door)
            def _():
                for owner in halves[1 - side]:
                    for copy in kv_direct(owner, door):
                        copy.wait_recv()
                    for dest in halves[side]:
                        if dest != door:
                            kv_onward(owner, dest).start()

        each_half(act)

    def finish_shared():
        for copy in shared_own():
            copy.wait()

        def act(side):
            for owner in halves[side]:
                @pl.when(owner != me)
                def _():
                    for copy in kv_direct(owner, me):
                        copy.wait_recv()

            @pl.when(me != doors[side])
            def _():
                for owner in halves[1 - side]:
                    kv_onward(owner, me).wait_recv()

        each_half(act)

    def drain_shared():
        def act(side):
            if len(halves[1 - side]):
                for copy in kv_direct(me, doors[1 - side]):
                    copy.wait_send()
            for dest in halves[side]:
                @pl.when(dest != me)
                def _():
                    for copy in kv_direct(me, dest):
                        copy.wait_send()

            @pl.when(me == doors[side])
            def _():
                for owner in halves[1 - side]:
                    for dest in halves[side]:
                        if dest != doors[side]:
                            kv_onward(owner, dest).wait_send()

        each_half(act)

    ahead = 4
    order = sorted(range(1, n), key=lambda d: abs(d - n / 2))

    def send_in(p):
        for d in order:
            for copy in in_copies(p, lax.rem(me + d, n), me, d):
                copy.start()
        for copy in own_copies(p):
            copy.start()

    first_half = lax.broadcasted_iota(jnp.int32, (span, LANES), 1) < head_size

    def prepare(block_keys, block_values):
        half = lax.broadcasted_iota(jnp.int32, (n * span, LANES), 1) < head_size
        ones = jnp.ones((n * span, LANES), jnp.bfloat16)
        usable = valid[...]
        k = block_keys()
        keys[...] = jnp.where(usable > 0.5, k, jnp.broadcast_to(k[0:1], k.shape))
        v = block_values()
        first_values[...] = jnp.where(half, v, ones) * usable
        second_values[...] = jnp.where(half, ones, v) * usable

    def attend_rows(queries):
        queries = queries * jnp.asarray(head_size ** (-0.5), jnp.bfloat16)
        zeros = jnp.zeros_like(queries)
        parts = []
        for own, values in ((jnp.where(first_half, queries, zeros), first_values),
                            (jnp.where(first_half, zeros, queries), second_values)):
            scores = lax.dot_general(own, keys[...], (((1,), (1,)), ((), ())), preferred_element_type=jnp.float32)
            probs = jnp.exp(scores - jnp.max(scores, axis=1, keepdims=True)).astype(jnp.bfloat16)
            parts.append(jnp.dot(probs, values[...], preferred_element_type=jnp.float32))
        summed = jnp.where(first_half, parts[0], parts[1])
        totals = pltpu.roll(jnp.where(first_half, parts[1], parts[0]), head_size, axis=1)
        return (summed / totals).astype(jnp.bfloat16)

    def attend_pair(p):
        for copy in own_copies(p):
            copy.wait()
        for d in range(1, n):
            for copy in in_copies(p, me, lax.rem(me + d, n), d):
                copy.wait_recv()
        if p + ahead < base:
            send_in(p + ahead)
        prepare(lambda: qkv[p, 1], lambda: qkv[p, 2])

        def one_block(j, _):
            dest = lax.rem(me + n // 2 + j, n)
            done[p, dest] = attend_rows(qkv[p, 0, rows_of(dest, 0, span), :])

            @pl.when(dest != me)
            def _():
                out_copy(p, dest, me, lax.rem(dest - me + n, n)).start()

            return 0

        lax.fori_loop(0, n, one_block, 0)
        own_out(p).start()

    def attend_shared():
        finish_shared()
        for e in range(extra):
            cols = pl.ds(e * LANES, LANES)
            prepare(lambda: shared_kv[0, :, cols], lambda: shared_kv[1, :, cols])
            attended[n * base + e] = attend_rows(shared_q[:, cols])

    def project(acc, full, rows, chosen, start, finish):
        left = jnp.concatenate([attended[c, rows, :] for c in chosen], axis=1)
        for at, size in column_tiles(width, 256):
            right = jnp.concatenate([full[pl.ds(c * LANES, LANES), pl.ds(at, size)] for c in chosen], axis=0)
            part = jnp.dot(left, right, preferred_element_type=jnp.float32)
            if not start:
                part = part + acc[:, pl.ds(at, size)]
            if finish is None:
                acc[:, pl.ds(at, size)] = part
            else:
                out, gate = finish
                out[:, pl.ds(at, size)] = (part * gates[0, pl.ds(gate, 1), pl.ds(at, size)]).astype(jnp.bfloat16)

    text_span = pl.ds(image_rows, text_rows)
    image_span = pl.ds(0, image_rows)

    if extra:
        start_shared()
    send_in(0)
    weights[0].advance(0)
    for p in range(1, min(ahead, base)):
        send_in(p)
    weights[1].advance(0)

    length_copy.wait()
    for b in range(n):
        at = lax.broadcasted_iota(jnp.int32, (span, LANES), 0)
        usable = (at >= image_rows) | (b * image_rows + at < length[0])
        valid[pl.ds(b * span, span), :] = jnp.where(usable, 1.0, 0.0).astype(jnp.bfloat16)

    for p in range(base):
        attend_pair(p)
        if p == 0:
            if extra:
                pass_shared()
            weights[0].advance(1)
        if p == min(1, base - 1):
            weights[1].advance(1)
        if p == max(0, base - 2) and extra:
            attend_shared()
    for level in range(2, len(weights[0].far) + 1):
        weights[0].advance(level)
    weights[0].finish()
    gates_copy.wait()
    started = bool(extra)
    if extra:
        project(image_acc, image_full, image_span, [n * base + e for e in range(extra)], True, None)
    for p in range(base):
        last = p == base - 1
        chosen = [b * base + p for b in range(n)]
        if last:
            for level in range(2, len(weights[1].far) + 1):
                weights[1].advance(level)
            weights[1].finish()
            if extra:
                project(text_acc, text_full, text_span, [n * base + e for e in range(extra)], True, None)
            for q in range(base - 1):
                project(text_acc, text_full, text_span, [b * base + q for b in range(n)], not extra and q == 0, None)
        own_out(p).wait()
        for d in range(1, n):
            out_copy(p, me, lax.rem(me + d, n), d).wait_recv()
        if last:
            project(text_acc, text_full, text_span, chosen, not extra and base == 1, (out_txt, 1))
        project(image_acc, image_full, image_span, chosen, not started, (out_img, 0) if last else None)
        started = True

    for p in range(base):
        for d in range(1, n):
            peer = lax.rem(me + d, n)
            for copy in in_copies(p, peer, me, d):
                copy.wait_send()
            out_copy(p, peer, me, d).wait_send()
    if extra:
        drain_shared()
    for weight in weights:
        weight.drain()


def store_kernel(image_in, text_in, image_out, text_out, sems):
    copies = [pltpu.make_async_copy(image_in, image_out, sems.at[0]), pltpu.make_async_copy(text_in, text_out, sems.at[1])]
    for copy in copies:
        copy.start()
    for copy in copies:
        copy.wait()


def store(outs):
    return pl.pallas_call(
        store_kernel,
        out_shape=tuple(jax.ShapeDtypeStruct(x.shape, x.dtype) for x in outs),
        in_specs=[pl.BlockSpec(memory_space=pl.ANY)] * 2,
        out_specs=(pl.BlockSpec(memory_space=pltpu.HBM),) * 2,
        scratch_shapes=[pltpu.SemaphoreType.DMA((2,))],
        name="store",
    )(*[pltpu.with_memory_space_constraint(x, pltpu.VMEM) for x in outs])


def per_device(image_tokens, text_tokens, lengths, image_weight, text_weight, gate_values):
    image_rows, text_rows, width = image_tokens.shape[1], text_tokens.shape[1], image_tokens.shape[2]
    n, group_count = lax.axis_size("blk"), lax.axis_size("grp")
    span = image_rows + text_rows
    pairs = width // LANES
    base, extra = divmod(pairs, n)
    bits = group_count.bit_length() - 1
    parts, masks = max(1, bits - 1), max(1, group_count // 2)
    dma = pltpu.SemaphoreType.DMA
    bf16, f32 = jnp.bfloat16, jnp.float32
    any_space = pl.BlockSpec(memory_space=pltpu.HBM)
    vmem = pl.BlockSpec(memory_space=pltpu.VMEM)
    wide = max(1, extra) * LANES
    outs = pl.pallas_call(
        functools.partial(block_kernel, n, group_count, width // HEADS),
        out_shape=(
            pltpu.VMEM((image_rows, width), bf16),
            pltpu.VMEM((text_rows, width), bf16),
        ),
        in_specs=[any_space] * 6,
        out_specs=(vmem, vmem),
        scratch_shapes=[
            pltpu.SMEM((1,), jnp.int32),
            pltpu.VMEM((1, 2, width), f32),
            pltpu.VMEM((base, 3, n * span, LANES), bf16),
            pltpu.VMEM((2, n * span, wide), bf16),
            pltpu.VMEM((span, wide), bf16),
            pltpu.VMEM((pairs, span, LANES), bf16),
            pltpu.VMEM((base, n, span, LANES), bf16),
            pltpu.VMEM((n * span, LANES), bf16),
            pltpu.VMEM((n * span, LANES), bf16),
            pltpu.VMEM((n * span, LANES), bf16),
            pltpu.VMEM((n * span, LANES), bf16),
            pltpu.VMEM((width, width), bf16),
            pltpu.VMEM((width, width), bf16),
            pltpu.VMEM((image_rows, width), f32),
            pltpu.VMEM((text_rows, width), f32),
            dma((base, n, 2)), dma((base, n, 2)), dma((base, 2)),
            dma((base, n)), dma((base, n)), dma((base,)),
            dma((n, 2)), dma((n, n)), dma((n, 2)), dma((2, 2)),
            dma((2,)), dma((2, parts, masks)), dma((2, parts, masks)), dma((2, parts, masks)), dma((2, parts, masks)),
            dma((2,)),
        ],
        compiler_params=pltpu.CompilerParams(
            collective_id=0, has_side_effects=True, vmem_limit_bytes=60 * 1024 * 1024
        ),
        name="attend",
    )(lengths, image_tokens, text_tokens, image_weight, text_weight, gate_values)
    return store(outs)


def solution(mesh):
    in_specs = (
        P(None, ("grp", "blk"), None),
        P(None, ("grp", "blk"), None),
        P("grp"),
        P("grp", None),
        P("grp", None),
        P("grp", None, None),
    )
    out_specs = (P(("grp", "blk"), None), P(("grp", "blk"), None))
    return jax.shard_map(
        per_device, mesh=mesh, in_specs=in_specs, out_specs=out_specs, check_vma=False
    )
```

```python
import functools

import jax
import jax.numpy as jnp
from jax import lax
from jax.experimental import pallas as pl
from jax.experimental.pallas import tpu as pltpu
from jax.sharding import PartitionSpec as P

HEADS = 38
LANES = 128
MESH = pl.DeviceIdType.MESH


def remote(src, dst, send, recv, axis, peer):
    return pltpu.make_async_remote_copy(
        src_ref=src, dst_ref=dst, send_sem=send, recv_sem=recv,
        device_id={axis: peer}, device_id_type=MESH)


def row_parts(rows, parts, unit):
    base, extra = divmod(rows // unit, parts)
    sizes = [(base + (1 if j < extra else 0)) * unit for j in range(parts)]
    return [(sum(sizes[:j]), sizes[j]) for j in range(parts) if sizes[j]]


def column_tiles(width, tile):
    return [(at, min(tile, width - at)) for at in range(0, width, tile)]


class WeightGather:
    def __init__(self, group_count, shard, full, send, far, near):
        self.shard, self.full = shard, full
        self.send, self.far_sem, self.near_sem = send, far, near
        self.rows = shard.shape[0]
        self.unit = 16 if self.rows % 16 == 0 else 8
        self.bits = group_count.bit_length() - 1
        self.far = list(range(1, self.bits))
        self.parts = row_parts(self.rows, max(1, len(self.far)), self.unit)
        self.me = lax.axis_index("grp")

    def flip(self, mask):
        at = self.me
        for k in range(self.bits):
            if mask >> k & 1:
                at = at + (1 - 2 * ((self.me // (1 << k)) % 2)) * (1 << k)
        return at

    def order(self, j):
        return self.far[j:] + self.far[:j] if self.far else []

    def masks(self, level):
        return [m for m in range(0, 1 << self.bits, 2) if bin(m).count("1") == level]

    def cuts(self, j, mask):
        first, size = self.parts[j]
        if mask.bit_count() < len(self.far):
            return [(first, size)]
        head = size * 2 // 3 // self.unit * self.unit
        return [(first, head), (first + head, size - head)]

    def piece(self, mask, rows):
        return self.full.at[pl.ds(pl.multiple_of(self.flip(mask) * self.rows + rows[0], self.unit), rows[1]), :]

    def source(self, mask, rows):
        return self.shard.at[pl.ds(*rows), :] if mask == 0 else self.piece(mask, rows)

    def shards(self, count):
        return self.full.at[pl.ds(0, count * self.rows), :]

    def own(self):
        return pltpu.make_async_copy(
            self.shard, self.full.at[pl.ds(pl.multiple_of(self.me * self.rows, self.unit), self.rows), :],
            self.near_sem.at[0])

    def wait(self, count, sem):
        pltpu.make_async_copy(self.shards(count), self.shards(count), sem).wait()

    def near(self, mask, rows):
        if self.bits:
            remote(self.source(mask, rows), self.piece(mask, rows), self.send, self.near_sem.at[mask.bit_count()],
                   "grp", self.flip(1)).start()

    def advance(self, level):
        if level > 0:
            self.wait(len(self.masks(level)), self.far_sem.at[level])
        for mask in self.masks(level):
            for j in range(len(self.parts)):
                order = self.order(j)
                done = max([order.index(k) for k in order if mask >> k & 1], default=-1)
                for k in order[done + 1:]:
                    there = mask | 1 << k
                    for i, rows in enumerate(self.cuts(j, there)):
                        remote(self.source(mask, rows), self.piece(mask, rows), self.send,
                               self.far_sem.at[level + 1 + i], "grp", self.flip(1 << k)).start()
                self.near(mask, self.parts[j])
        if level == 0:
            self.own().start()

    def advance_last(self, i):
        level = len(self.far)
        if level == 0:
            return
        (mask,) = self.masks(level)
        ranges = [self.cuts(j, mask)[i] for j in range(len(self.parts))]
        ref = self.full.at[pl.ds(0, sum(size for _, size in ranges)), :]
        pltpu.make_async_copy(ref, ref, self.far_sem.at[level + i]).wait()
        for rows in ranges:
            self.near(mask, rows)

    def finish(self, level):
        if level <= len(self.far):
            self.wait((len(self.masks(level)) if self.bits else 0) + (level == 0), self.near_sem.at[level])

    def drain(self):
        far = 1 << len(self.far)
        if self.bits:
            self.wait(far - 1 + far, self.send)


def block_kernel(
    n, group_count, head_size,
    length_in, img, txt, image_shard, text_shard, gates_in, out_img, out_txt,
    length, gates,
    qkv, shared_kv, shared_q, attended, done, keys, first_values, second_values, valid, image_full, text_full,
    image_acc, text_acc,
    in_send, in_recv, out_send, out_recv, kv_send, kv_recv, shared_local, w_send, w_far, w_near, small_local,
):
    me = lax.axis_index("blk")
    image_rows, text_rows, width = img.shape[1], txt.shape[1], img.shape[2]
    span = image_rows + text_rows
    pairs = width // LANES
    base, extra = divmod(pairs, n)
    streams = ((img, 0, image_rows), (txt, image_rows, text_rows))

    weights = [
        WeightGather(group_count, shard, full, w_send.at[i], w_far.at[i], w_near.at[i])
        for i, (shard, full) in enumerate(((image_shard, image_full), (text_shard, text_full)))
    ]

    length_copy = pltpu.make_async_copy(length_in, length, small_local.at[0])
    gates_copy = pltpu.make_async_copy(gates_in, gates, small_local.at[1])
    length_copy.start()
    gates_copy.start()

    barrier = pltpu.get_barrier_semaphore()
    for d in range(1, n):
        pl.semaphore_signal(barrier, inc=1, device_id={"blk": lax.rem(me + d, n)}, device_id_type=MESH)
    for k in range(weights[0].bits):
        pl.semaphore_signal(barrier, inc=1, device_id={"grp": weights[0].flip(1 << k)}, device_id_type=MESH)
    pl.semaphore_wait(barrier, n - 1 + weights[0].bits)

    def columns(b, p):
        return pl.ds(pl.multiple_of((b * base + p) * LANES, LANES), LANES)

    def rows_of(b, first, count):
        return pl.ds(pl.multiple_of(b * span + first, 16), count)

    def in_copies(p, dest):
        return [
            remote(src.at[:, :, columns(dest, p)], qkv.at[p, :, rows_of(me, first, count), :],
                   in_send, in_recv.at[p], "blk", dest)
            for src, first, count in streams
        ]

    def own_copies(p):
        return [
            pltpu.make_async_copy(
                src.at[:, :, columns(me, p)], qkv.at[p, :, rows_of(me, first, count), :], in_recv.at[p])
            for src, first, count in streams
        ]

    def out_copy(p, dest):
        return remote(done.at[p, dest], attended.at[me * base + p], out_send, out_recv.at[p], "blk", dest)

    def own_out(p):
        return pltpu.make_async_copy(done.at[p, me], attended.at[me * base + p], out_recv.at[p])

    def wait_bytes(ref, sem):
        pltpu.make_async_copy(ref, ref, sem).wait()

    shared_cols = pl.ds(n * base * LANES, extra * LANES)

    middle = n // 2
    halves = (range(middle), range(middle, n))
    doors = (middle - 1, middle)

    def kv_direct(dest, across):
        return [
            remote(src.at[pl.ds(1, 2), :, shared_cols], shared_kv.at[:, rows_of(me, first, count), :],
                   kv_send, kv_recv.at[across], "blk", dest)
            for src, first, count in streams
        ]

    def kv_onward(owner, dest):
        block = shared_kv.at[:, rows_of(owner, 0, span), :]
        return remote(block, block, kv_send, kv_recv.at[1], "blk", dest)

    def kv_wait(blocks, sem):
        if blocks:
            wait_bytes(shared_kv.at[:, pl.ds(0, blocks * span), :], sem)

    def shared_own():
        copies = []
        for src, first, count in streams:
            copies.append(pltpu.make_async_copy(
                src.at[pl.ds(1, 2), :, shared_cols], shared_kv.at[:, rows_of(me, first, count), :], kv_recv.at[0]))
            copies.append(pltpu.make_async_copy(
                src.at[0, :, shared_cols], shared_q.at[pl.ds(first, count), :], shared_local))
        return copies

    def each_half(act):
        for side in range(2):
            if len(halves[side]):
                @pl.when((me < middle) if side == 0 else (me >= middle))
                def _():
                    act(side)

    def start_shared():
        def act(side):
            if len(halves[1 - side]):
                for copy in kv_direct(doors[1 - side], 1):
                    copy.start()
            for dest in halves[side]:
                @pl.when(dest != me)
                def _():
                    for copy in kv_direct(dest, 0):
                        copy.start()

        each_half(act)
        for copy in shared_own():
            copy.start()

    def pass_shared():
        def act(side):
            @pl.when(me == doors[side])
            def _():
                kv_wait(len(halves[1 - side]), kv_recv.at[1])
                for owner in halves[1 - side]:
                    for dest in halves[side]:
                        if dest != doors[side]:
                            kv_onward(owner, dest).start()

        each_half(act)

    def finish_shared():
        wait_bytes(shared_q, shared_local)

        def act(side):
            kv_wait(len(halves[side]), kv_recv.at[0])

            @pl.when(me != doors[side])
            def _():
                kv_wait(len(halves[1 - side]), kv_recv.at[1])

        each_half(act)

    def drain_shared():
        def act(side):
            own, other = len(halves[side]), len(halves[1 - side])
            kv_wait(own - 1 + (other > 0), kv_send)

            @pl.when(me == doors[side])
            def _():
                for _ in range(own - 1):
                    kv_wait(other, kv_send)

        each_half(act)

    order = sorted(range(1, n), key=lambda d: abs(d - n / 2))

    def send_in(p):
        for d in order:
            for copy in in_copies(p, lax.rem(me + d, n)):
                copy.start()
        for copy in own_copies(p):
            copy.start()

    first_half = lax.broadcasted_iota(jnp.int32, (span, LANES), 1) < head_size

    def prepare(block_keys, block_values):
        half = lax.broadcasted_iota(jnp.int32, (n * span, LANES), 1) < head_size
        ones = jnp.ones((n * span, LANES), jnp.bfloat16)
        usable = valid[...]
        k = block_keys()
        keys[...] = jnp.where(usable > 0.5, k, jnp.broadcast_to(k[0:1], k.shape))
        v = block_values()
        first_values[...] = jnp.where(half, v, ones) * usable
        second_values[...] = jnp.where(half, ones, v) * usable

    def attend_rows(queries):
        queries = queries * jnp.asarray(head_size ** (-0.5), jnp.bfloat16)
        zeros = jnp.zeros_like(queries)
        parts = []
        for own, values in ((jnp.where(first_half, queries, zeros), first_values),
                            (jnp.where(first_half, zeros, queries), second_values)):
            scores = lax.dot_general(own, keys[...], (((1,), (1,)), ((), ())), preferred_element_type=jnp.float32)
            probs = jnp.exp(scores - jnp.max(scores, axis=1, keepdims=True)).astype(jnp.bfloat16)
            parts.append(jnp.dot(probs, values[...], preferred_element_type=jnp.float32))
        summed = jnp.where(first_half, parts[0], parts[1])
        totals = pltpu.roll(jnp.where(first_half, parts[1], parts[0]), head_size, axis=1)
        return (summed / totals).astype(jnp.bfloat16)

    def attend_pair(p):
        wait_bytes(qkv.at[p], in_recv.at[p])
        prepare(lambda: qkv[p, 1], lambda: qkv[p, 2])

        def one_block(j, _):
            dest = lax.rem(me + n // 2 + j, n)
            done[p, dest] = attend_rows(qkv[p, 0, rows_of(dest, 0, span), :])

            @pl.when(dest != me)
            def _():
                out_copy(p, dest).start()

            return 0

        lax.fori_loop(0, n, one_block, 0)
        own_out(p).start()

    def attend_shared():
        finish_shared()
        for e in range(extra):
            cols = pl.ds(e * LANES, LANES)
            prepare(lambda: shared_kv[0, :, cols], lambda: shared_kv[1, :, cols])
            attended[n * base + e] = attend_rows(shared_q[:, cols])

    def project(acc, full, rows, chosen, start, finish):
        left = jnp.concatenate([attended[c, rows, :] for c in chosen], axis=1)
        for at, size in column_tiles(width, 256):
            right = jnp.concatenate([full[pl.ds(c * LANES, LANES), pl.ds(at, size)] for c in chosen], axis=0)
            part = jnp.dot(left, right, preferred_element_type=jnp.float32)
            if not start:
                part = part + acc[:, pl.ds(at, size)]
            if finish is None:
                acc[:, pl.ds(at, size)] = part
            else:
                out, gate = finish
                out[:, pl.ds(at, size)] = (part * gates[0, pl.ds(gate, 1), pl.ds(at, size)]).astype(jnp.bfloat16)

    def text_step(c):
        part = jnp.dot(attended[c, text_span, :], text_full[pl.ds(pl.multiple_of(c * LANES, LANES), LANES), :],
                       preferred_element_type=jnp.float32)
        text_acc[...] += part

    def early_text(first, stride, count):
        def step(i, _):
            c = first + stride * i

            @pl.when(lax.rem(c - late_first + pairs, pairs) >= late_pairs)
            def _():
                text_step(c)

            return 0

        lax.fori_loop(0, count, step, 0)

    late_rows = 2 * weights[1].rows if weights[1].bits else weights[1].rows
    late_pairs = min(pairs, -(-late_rows // LANES) + 1)
    late_first = weights[1].flip(sum(1 << k for k in weights[1].far)) // 2 * late_rows // LANES

    text_span = pl.ds(image_rows, text_rows)
    image_span = pl.ds(0, image_rows)

    if extra:
        start_shared()
    send_in(0)
    weights[0].advance(0)
    for p in range(1, base):
        send_in(p)
    weights[1].advance(0)

    length_copy.wait()
    for b in range(n):
        at = lax.broadcasted_iota(jnp.int32, (span, LANES), 0)
        usable = (at >= image_rows) | (b * image_rows + at < length[0])
        valid[pl.ds(b * span, span), :] = jnp.where(usable, 1.0, 0.0).astype(jnp.bfloat16)

    far_levels = len(weights[0].far)

    def advance(i, level):
        if level < far_levels:
            weights[i].advance(level)

    is_door = (me == doors[0]) | (me == doors[1])
    for p in range(base):
        if p == base - 1:
            if extra:
                pl.when(is_door)(attend_shared)
            for level in range(2, far_levels):
                weights[0].advance(level)
            for i in range(2):
                weights[0].advance_last(i)
        attend_pair(p)
        if p == 0:
            if extra:
                pass_shared()
            advance(0, 1)
        if p == min(1, base - 1):
            advance(1, 1)
    if extra:
        pl.when(jnp.logical_not(is_door))(attend_shared)
    for level in range(far_levels + 1):
        weights[0].finish(level)
    gates_copy.wait()

    def wait_out(p):
        wait_bytes(attended.at[pl.ds(0, n)], out_recv.at[p])

    for level in range(2, far_levels):
        weights[1].advance(level)
    for level in range(far_levels):
        weights[1].finish(level)
    text_acc[...] = jnp.zeros_like(text_acc)
    started = bool(extra)
    if extra:
        project(image_acc, image_full, image_span, [n * base + e for e in range(extra)], True, None)
        early_text(n * base, 1, extra)
    for p in range(base):
        wait_out(p)
        last = p == base - 1
        if last:
            if base == 1:
                weights[1].advance_last(0)
            weights[1].advance_last(1)
        project(image_acc, image_full, image_span, [b * base + p for b in range(n)], not started,
                (out_img, 0) if last else None)
        if p == base - 2:
            weights[1].advance_last(0)
        early_text(p, base, n)
        started = True
    weights[1].finish(far_levels)
    for i in range(late_pairs):
        text_step(lax.rem(late_first + i, pairs))
    out_txt[...] = (text_acc[...] * gates[0, 1:2, :]).astype(jnp.bfloat16)

    wait_bytes(qkv.at[:, :, pl.ds(0, (n - 1) * span), :], in_send)
    for _ in range(base):
        wait_bytes(attended.at[pl.ds(0, n - 1)], out_send)
    if extra:
        drain_shared()
    for weight in weights:
        weight.drain()


def store_kernel(image_in, text_in, image_out, text_out, sems):
    copies = [pltpu.make_async_copy(image_in, image_out, sems.at[0]), pltpu.make_async_copy(text_in, text_out, sems.at[1])]
    for copy in copies:
        copy.start()
    for copy in copies:
        copy.wait()


def store(outs):
    return pl.pallas_call(
        store_kernel,
        out_shape=tuple(jax.ShapeDtypeStruct(x.shape, x.dtype) for x in outs),
        in_specs=[pl.BlockSpec(memory_space=pl.ANY)] * 2,
        out_specs=(pl.BlockSpec(memory_space=pltpu.HBM),) * 2,
        scratch_shapes=[pltpu.SemaphoreType.DMA((2,))],
        name="store",
    )(*[pltpu.with_memory_space_constraint(x, pltpu.VMEM) for x in outs])


def per_device(image_tokens, text_tokens, lengths, image_weight, text_weight, gate_values):
    image_rows, text_rows, width = image_tokens.shape[1], text_tokens.shape[1], image_tokens.shape[2]
    n, group_count = lax.axis_size("blk"), lax.axis_size("grp")
    span = image_rows + text_rows
    pairs = width // LANES
    base, extra = divmod(pairs, n)
    bits = group_count.bit_length() - 1
    levels = max(1, bits)
    dma = pltpu.SemaphoreType.DMA
    bf16, f32 = jnp.bfloat16, jnp.float32
    any_space = pl.BlockSpec(memory_space=pltpu.HBM)
    vmem = pl.BlockSpec(memory_space=pltpu.VMEM)
    wide = max(1, extra) * LANES
    outs = pl.pallas_call(
        functools.partial(block_kernel, n, group_count, width // HEADS),
        out_shape=(
            pltpu.VMEM((image_rows, width), bf16),
            pltpu.VMEM((text_rows, width), bf16),
        ),
        in_specs=[any_space] * 6,
        out_specs=(vmem, vmem),
        scratch_shapes=[
            pltpu.SMEM((1,), jnp.int32),
            pltpu.VMEM((1, 2, width), f32),
            pltpu.VMEM((base, 3, n * span, LANES), bf16),
            pltpu.VMEM((2, n * span, wide), bf16),
            pltpu.VMEM((span, wide), bf16),
            pltpu.VMEM((pairs, span, LANES), bf16),
            pltpu.VMEM((base, n, span, LANES), bf16),
            pltpu.VMEM((n * span, LANES), bf16),
            pltpu.VMEM((n * span, LANES), bf16),
            pltpu.VMEM((n * span, LANES), bf16),
            pltpu.VMEM((n * span, LANES), bf16),
            pltpu.VMEM((width, width), bf16),
            pltpu.VMEM((width, width), bf16),
            pltpu.VMEM((image_rows, width), f32),
            pltpu.VMEM((text_rows, width), f32),
            dma, dma((base,)), dma, dma((base,)), dma, dma((2,)), dma,
            dma((2,)), dma((2, levels + 1)), dma((2, levels)), dma((2,)),
        ],
        compiler_params=pltpu.CompilerParams(
            collective_id=0, has_side_effects=True, vmem_limit_bytes=60 * 1024 * 1024
        ),
        name="attend",
    )(lengths, image_tokens, text_tokens, image_weight, text_weight, gate_values)
    return store(outs)


def solution(mesh):
    in_specs = (
        P(None, ("grp", "blk"), None),
        P(None, ("grp", "blk"), None),
        P("grp"),
        P("grp", None),
        P("grp", None),
        P("grp", None, None),
    )
    out_specs = (P(("grp", "blk"), None), P(("grp", "blk"), None))
    return jax.shard_map(
        per_device, mesh=mesh, in_specs=in_specs, out_specs=out_specs, check_vma=False
    )
```

```python
import functools

import jax
import jax.numpy as jnp
from jax import lax
from jax.experimental import pallas as pl
from jax.experimental.pallas import tpu as pltpu
from jax.sharding import PartitionSpec as P

HEADS = 38
LANES = 128
MESH = pl.DeviceIdType.MESH


def remote(src, dst, send, recv, axis, peer):
    return pltpu.make_async_remote_copy(
        src_ref=src, dst_ref=dst, send_sem=send, recv_sem=recv,
        device_id={axis: peer}, device_id_type=MESH)


def row_parts(rows, parts, unit):
    base, extra = divmod(rows // unit, parts)
    sizes = [(base + (1 if j < extra else 0)) * unit for j in range(parts)]
    return [(sum(sizes[:j]), sizes[j]) for j in range(parts) if sizes[j]]


def column_tiles(width, tile):
    return [(at, min(tile, width - at)) for at in range(0, width, tile)]


class WeightGather:
    def __init__(self, group_count, shard, full, send, far, near):
        self.shard, self.full = shard, full
        self.send, self.far_sem, self.near_sem = send, far, near
        self.rows = shard.shape[0]
        self.unit = 16 if self.rows % 16 == 0 else 8
        self.bits = group_count.bit_length() - 1
        self.far = list(range(1, self.bits))
        self.parts = row_parts(self.rows, max(1, len(self.far)), self.unit)
        self.me = lax.axis_index("grp")

    def flip(self, mask):
        at = self.me
        for k in range(self.bits):
            if mask >> k & 1:
                at = at + (1 - 2 * ((self.me // (1 << k)) % 2)) * (1 << k)
        return at

    def order(self, j):
        return self.far[j:] + self.far[:j] if self.far else []

    def masks(self, level):
        return [m for m in range(0, 1 << self.bits, 2) if bin(m).count("1") == level]

    def cuts(self, j, mask):
        first, size = self.parts[j]
        if mask.bit_count() < len(self.far):
            return [(first, size)]
        head = size * 2 // 3 // self.unit * self.unit
        return [(first, head), (first + head, size - head)]

    def piece(self, mask, rows):
        return self.full.at[pl.ds(pl.multiple_of(self.flip(mask) * self.rows + rows[0], self.unit), rows[1]), :]

    def source(self, mask, rows):
        return self.shard.at[pl.ds(*rows), :] if mask == 0 else self.piece(mask, rows)

    def shards(self, count):
        return self.full.at[pl.ds(0, count * self.rows), :]

    def own(self):
        return pltpu.make_async_copy(
            self.shard, self.full.at[pl.ds(pl.multiple_of(self.me * self.rows, self.unit), self.rows), :],
            self.near_sem.at[0])

    def wait(self, count, sem):
        pltpu.make_async_copy(self.shards(count), self.shards(count), sem).wait()

    def near(self, mask, rows):
        if self.bits:
            remote(self.source(mask, rows), self.piece(mask, rows), self.send, self.near_sem.at[mask.bit_count()],
                   "grp", self.flip(1)).start()

    def advance(self, level):
        if level > 0:
            self.wait(len(self.masks(level)), self.far_sem.at[level])
        for mask in self.masks(level):
            for j in range(len(self.parts)):
                order = self.order(j)
                done = max([order.index(k) for k in order if mask >> k & 1], default=-1)
                for k in order[done + 1:]:
                    there = mask | 1 << k
                    for i, rows in enumerate(self.cuts(j, there)):
                        remote(self.source(mask, rows), self.piece(mask, rows), self.send,
                               self.far_sem.at[level + 1 + i], "grp", self.flip(1 << k)).start()
                self.near(mask, self.parts[j])
        if level == 0:
            self.own().start()

    def advance_last(self, i):
        level = len(self.far)
        if level == 0:
            return
        (mask,) = self.masks(level)
        ranges = [self.cuts(j, mask)[i] for j in range(len(self.parts))]
        ref = self.full.at[pl.ds(0, sum(size for _, size in ranges)), :]
        pltpu.make_async_copy(ref, ref, self.far_sem.at[level + i]).wait()
        for rows in ranges:
            self.near(mask, rows)

    def finish(self, level):
        if level <= len(self.far):
            self.wait((len(self.masks(level)) if self.bits else 0) + (level == 0), self.near_sem.at[level])

    def drain(self):
        far = 1 << len(self.far)
        if self.bits:
            self.wait(far - 1 + far, self.send)


def block_kernel(
    n, group_count, head_size,
    length_in, img, txt, image_shard, text_shard, gates_in, out_img, out_txt,
    length, gates,
    qkv, shared_kv, shared_q, attended, done, keys, first_values, second_values, valid, image_full, text_full,
    image_acc, text_acc,
    in_send, in_recv, out_send, out_recv, kv_send, kv_recv, shared_local, w_send, w_far, w_near, small_local,
):
    me = lax.axis_index("blk")
    image_rows, text_rows, width = img.shape[1], txt.shape[1], img.shape[2]
    span = image_rows + text_rows
    pairs = width // LANES
    base, extra = divmod(pairs, n)
    streams = ((img, 0, image_rows), (txt, image_rows, text_rows))

    weights = [
        WeightGather(group_count, shard, full, w_send.at[i], w_far.at[i], w_near.at[i])
        for i, (shard, full) in enumerate(((image_shard, image_full), (text_shard, text_full)))
    ]

    length_copy = pltpu.make_async_copy(length_in, length, small_local.at[0])
    gates_copy = pltpu.make_async_copy(gates_in, gates, small_local.at[1])
    length_copy.start()
    gates_copy.start()

    barrier = pltpu.get_barrier_semaphore()
    for d in range(1, n):
        pl.semaphore_signal(barrier, inc=1, device_id={"blk": lax.rem(me + d, n)}, device_id_type=MESH)
    for k in range(weights[0].bits):
        pl.semaphore_signal(barrier, inc=1, device_id={"grp": weights[0].flip(1 << k)}, device_id_type=MESH)
    pl.semaphore_wait(barrier, n - 1 + weights[0].bits)

    def columns(b, p):
        return pl.ds(pl.multiple_of((b * base + p) * LANES, LANES), LANES)

    def rows_of(b, first, count):
        return pl.ds(pl.multiple_of(b * span + first, 16), count)

    def in_copies(p, dest):
        return [
            remote(src.at[:, :, columns(dest, p)], qkv.at[p, :, rows_of(me, first, count), :],
                   in_send, in_recv.at[p], "blk", dest)
            for src, first, count in streams
        ]

    def own_copies(p):
        return [
            pltpu.make_async_copy(
                src.at[:, :, columns(me, p)], qkv.at[p, :, rows_of(me, first, count), :], in_recv.at[p])
            for src, first, count in streams
        ]

    middle = n // 2
    split = n % 2 == 0

    def out_copy(p, dest):
        across = jnp.where((me < middle) == (dest < middle), 0, 1) if split else 0
        return remote(done.at[p, dest], attended.at[me * base + p], out_send, out_recv.at[p, across], "blk", dest)

    def own_out(p):
        return pltpu.make_async_copy(done.at[p, me], attended.at[me * base + p], out_recv.at[p, 0])

    def wait_bytes(ref, sem):
        pltpu.make_async_copy(ref, ref, sem).wait()

    shared_cols = pl.ds(n * base * LANES, extra * LANES)

    halves = (range(middle), range(middle, n))
    doors = (middle - 1, middle)

    def kv_direct(dest, across):
        return [
            remote(src.at[pl.ds(1, 2), :, shared_cols], shared_kv.at[:, rows_of(me, first, count), :],
                   kv_send, kv_recv.at[across], "blk", dest)
            for src, first, count in streams
        ]

    def kv_onward(owner, dest):
        block = shared_kv.at[:, rows_of(owner, 0, span), :]
        return remote(block, block, kv_send, kv_recv.at[1], "blk", dest)

    def kv_wait(blocks, sem):
        if blocks:
            wait_bytes(shared_kv.at[:, pl.ds(0, blocks * span), :], sem)

    def shared_own():
        copies = []
        for src, first, count in streams:
            copies.append(pltpu.make_async_copy(
                src.at[pl.ds(1, 2), :, shared_cols], shared_kv.at[:, rows_of(me, first, count), :], kv_recv.at[0]))
            copies.append(pltpu.make_async_copy(
                src.at[0, :, shared_cols], shared_q.at[pl.ds(first, count), :], shared_local))
        return copies

    def each_half(act):
        for side in range(2):
            if len(halves[side]):
                @pl.when((me < middle) if side == 0 else (me >= middle))
                def _():
                    act(side)

    def start_shared():
        def act(side):
            if len(halves[1 - side]):
                for copy in kv_direct(doors[1 - side], 1):
                    copy.start()
            for dest in halves[side]:
                @pl.when(dest != me)
                def _():
                    for copy in kv_direct(dest, 0):
                        copy.start()

        each_half(act)
        for copy in shared_own():
            copy.start()

    def pass_shared():
        def act(side):
            @pl.when(me == doors[side])
            def _():
                kv_wait(len(halves[1 - side]), kv_recv.at[1])
                for owner in halves[1 - side]:
                    for dest in halves[side]:
                        if dest != doors[side]:
                            kv_onward(owner, dest).start()

        each_half(act)

    def finish_shared():
        wait_bytes(shared_q, shared_local)

        def act(side):
            kv_wait(len(halves[side]), kv_recv.at[0])

            @pl.when(me != doors[side])
            def _():
                kv_wait(len(halves[1 - side]), kv_recv.at[1])

        each_half(act)

    def drain_shared():
        def act(side):
            own, other = len(halves[side]), len(halves[1 - side])
            kv_wait(own - 1 + (other > 0), kv_send)

            @pl.when(me == doors[side])
            def _():
                for _ in range(own - 1):
                    kv_wait(other, kv_send)

        each_half(act)

    order = sorted(range(1, n), key=lambda d: abs(d - n / 2))

    def send_in(p):
        for d in order:
            for copy in in_copies(p, lax.rem(me + d, n)):
                copy.start()
        for copy in own_copies(p):
            copy.start()

    first_half = lax.broadcasted_iota(jnp.int32, (span, LANES), 1) < head_size

    def prepare(block_keys, block_values):
        half = lax.broadcasted_iota(jnp.int32, (n * span, LANES), 1) < head_size
        ones = jnp.ones((n * span, LANES), jnp.bfloat16)
        usable = valid[...]
        k = block_keys()
        keys[...] = jnp.where(usable > 0.5, k, jnp.broadcast_to(k[0:1], k.shape))
        v = block_values()
        first_values[...] = jnp.where(half, v, ones) * usable
        second_values[...] = jnp.where(half, ones, v) * usable

    def attend_rows(queries):
        queries = queries * jnp.asarray(head_size ** (-0.5), jnp.bfloat16)
        zeros = jnp.zeros_like(queries)
        parts = []
        for own, values in ((jnp.where(first_half, queries, zeros), first_values),
                            (jnp.where(first_half, zeros, queries), second_values)):
            scores = lax.dot_general(own, keys[...], (((1,), (1,)), ((), ())), preferred_element_type=jnp.float32)
            probs = jnp.exp(scores - jnp.max(scores, axis=1, keepdims=True)).astype(jnp.bfloat16)
            parts.append(jnp.dot(probs, values[...], preferred_element_type=jnp.float32))
        summed = jnp.where(first_half, parts[0], parts[1])
        totals = pltpu.roll(jnp.where(first_half, parts[1], parts[0]), head_size, axis=1)
        return (summed / totals).astype(jnp.bfloat16)

    def attend_pair(p):
        wait_bytes(qkv.at[p], in_recv.at[p])
        prepare(lambda: qkv[p, 1], lambda: qkv[p, 2])

        def one_block(j, _):
            dest = lax.rem(me + n // 2 + j, n)
            done[p, dest] = attend_rows(qkv[p, 0, rows_of(dest, 0, span), :])

            @pl.when(dest != me)
            def _():
                out_copy(p, dest).start()

            return 0

        lax.fori_loop(0, n, one_block, 0)
        own_out(p).start()

    def attend_shared():
        finish_shared()
        for e in range(extra):
            cols = pl.ds(e * LANES, LANES)
            prepare(lambda: shared_kv[0, :, cols], lambda: shared_kv[1, :, cols])
            attended[n * base + e] = attend_rows(shared_q[:, cols])

    def project(acc, full, rows, chosen, start, finish):
        left = jnp.concatenate([attended[c, rows, :] for c in chosen], axis=1)
        for at, size in column_tiles(width, 256):
            right = jnp.concatenate([full[pl.ds(pl.multiple_of(c * LANES, LANES), LANES), pl.ds(at, size)] for c in chosen], axis=0)
            part = jnp.dot(left, right, preferred_element_type=jnp.float32)
            if not start:
                part = part + acc[:, pl.ds(at, size)]
            if finish is None:
                acc[:, pl.ds(at, size)] = part
            else:
                out, gate = finish
                out[:, pl.ds(at, size)] = (part * gates[0, pl.ds(gate, 1), pl.ds(at, size)]).astype(jnp.bfloat16)

    def text_step(c):
        part = jnp.dot(attended[c, text_span, :], text_full[pl.ds(pl.multiple_of(c * LANES, LANES), LANES), :],
                       preferred_element_type=jnp.float32)
        text_acc[...] += part

    def early_text(first, stride, count):
        def step(i, _):
            c = first + stride * i

            @pl.when(lax.rem(c - late_first + pairs, pairs) >= late_pairs)
            def _():
                text_step(c)

            return 0

        lax.fori_loop(0, count, step, 0)

    late_rows = 2 * weights[1].rows if weights[1].bits else weights[1].rows
    late_pairs = min(pairs, -(-late_rows // LANES) + 1)
    late_first = weights[1].flip(sum(1 << k for k in weights[1].far)) // 2 * late_rows // LANES

    text_span = pl.ds(image_rows, text_rows)
    image_span = pl.ds(0, image_rows)

    if extra:
        start_shared()
    send_in(0)
    weights[0].advance(0)
    for p in range(1, base):
        send_in(p)
    weights[1].advance(0)

    length_copy.wait()
    for b in range(n):
        at = lax.broadcasted_iota(jnp.int32, (span, LANES), 0)
        usable = (at >= image_rows) | (b * image_rows + at < length[0])
        valid[pl.ds(b * span, span), :] = jnp.where(usable, 1.0, 0.0).astype(jnp.bfloat16)

    far_levels = len(weights[0].far)

    def advance(i, level):
        if level < far_levels:
            weights[i].advance(level)

    is_door = (me == doors[0]) | (me == doors[1])
    for p in range(base):
        if p == base - 1:
            if extra:
                pl.when(is_door)(attend_shared)
            for level in range(2, far_levels):
                weights[0].advance(level)
            for i in range(2):
                weights[0].advance_last(i)
        attend_pair(p)
        if p == 0:
            if extra:
                pass_shared()
            advance(0, 1)
        if p == min(1, base - 1):
            advance(1, 1)
    if extra:
        pl.when(jnp.logical_not(is_door))(attend_shared)
    for level in range(far_levels + 1):
        weights[0].finish(level)
    gates_copy.wait()

    def wait_out(p, across):
        wait_bytes(attended.at[pl.ds(0, n // 2 if split else n)], out_recv.at[p, across])

    for level in range(2, far_levels):
        weights[1].advance(level)
    for level in range(far_levels):
        weights[1].finish(level)
    text_acc[...] = jnp.zeros_like(text_acc)
    started = bool(extra)
    if extra:
        project(image_acc, image_full, image_span, [n * base + e for e in range(extra)], True, None)
        early_text(n * base, 1, extra)
    if base < 3:
        weights[1].advance_last(0)
    near_first = jnp.where(me < middle, 0, middle) if split else 0
    for p in range(base):
        last = p == base - 1
        if p >= base - 2 and split:
            groups = [(near_first, n // 2, 0), (middle - near_first, n // 2, 1)]
        else:
            groups = [(0, n, 0)]
        for first, count, across in groups:
            wait_out(p, across)
            if split and len(groups) == 1:
                wait_out(p, 1)
            if p == max(0, base - 2) and across == len(groups) - 1:
                weights[1].advance_last(1)
            ends = last and across == len(groups) - 1
            project(image_acc, image_full, image_span, [(first + b) * base + p for b in range(count)], not started,
                    (out_img, 0) if ends else None)
            started = True
            early_text(first * base + p, base, count)
        if p == base - 3:
            weights[1].advance_last(0)
    weights[1].finish(far_levels)
    for i in range(late_pairs):
        text_step(lax.rem(late_first + i, pairs))
    out_txt[...] = (text_acc[...] * gates[0, 1:2, :]).astype(jnp.bfloat16)

    wait_bytes(qkv.at[:, :, pl.ds(0, (n - 1) * span), :], in_send)
    for _ in range(base):
        wait_bytes(attended.at[pl.ds(0, n - 1)], out_send)
    if extra:
        drain_shared()
    for weight in weights:
        weight.drain()


def store_kernel(image_in, text_in, image_out, text_out, sems):
    copies = [pltpu.make_async_copy(image_in, image_out, sems.at[0]), pltpu.make_async_copy(text_in, text_out, sems.at[1])]
    for copy in copies:
        copy.start()
    for copy in copies:
        copy.wait()


def store(outs):
    return pl.pallas_call(
        store_kernel,
        out_shape=tuple(jax.ShapeDtypeStruct(x.shape, x.dtype) for x in outs),
        in_specs=[pl.BlockSpec(memory_space=pl.ANY)] * 2,
        out_specs=(pl.BlockSpec(memory_space=pltpu.HBM),) * 2,
        scratch_shapes=[pltpu.SemaphoreType.DMA((2,))],
        name="store",
    )(*[pltpu.with_memory_space_constraint(x, pltpu.VMEM) for x in outs])


def per_device(image_tokens, text_tokens, lengths, image_weight, text_weight, gate_values):
    image_rows, text_rows, width = image_tokens.shape[1], text_tokens.shape[1], image_tokens.shape[2]
    n, group_count = lax.axis_size("blk"), lax.axis_size("grp")
    span = image_rows + text_rows
    pairs = width // LANES
    base, extra = divmod(pairs, n)
    bits = group_count.bit_length() - 1
    levels = max(1, bits)
    dma = pltpu.SemaphoreType.DMA
    bf16, f32 = jnp.bfloat16, jnp.float32
    any_space = pl.BlockSpec(memory_space=pltpu.HBM)
    vmem = pl.BlockSpec(memory_space=pltpu.VMEM)
    wide = max(1, extra) * LANES
    outs = pl.pallas_call(
        functools.partial(block_kernel, n, group_count, width // HEADS),
        out_shape=(
            pltpu.VMEM((image_rows, width), bf16),
            pltpu.VMEM((text_rows, width), bf16),
        ),
        in_specs=[any_space] * 6,
        out_specs=(vmem, vmem),
        scratch_shapes=[
            pltpu.SMEM((1,), jnp.int32),
            pltpu.VMEM((1, 2, width), f32),
            pltpu.VMEM((base, 3, n * span, LANES), bf16),
            pltpu.VMEM((2, n * span, wide), bf16),
            pltpu.VMEM((span, wide), bf16),
            pltpu.VMEM((pairs, span, LANES), bf16),
            pltpu.VMEM((base, n, span, LANES), bf16),
            pltpu.VMEM((n * span, LANES), bf16),
            pltpu.VMEM((n * span, LANES), bf16),
            pltpu.VMEM((n * span, LANES), bf16),
            pltpu.VMEM((n * span, LANES), bf16),
            pltpu.VMEM((width, width), bf16),
            pltpu.VMEM((width, width), bf16),
            pltpu.VMEM((image_rows, width), f32),
            pltpu.VMEM((text_rows, width), f32),
            dma, dma((base,)), dma, dma((base, 2)), dma, dma((2,)), dma,
            dma((2,)), dma((2, levels + 1)), dma((2, levels)), dma((2,)),
        ],
        compiler_params=pltpu.CompilerParams(
            collective_id=0, has_side_effects=True, vmem_limit_bytes=60 * 1024 * 1024
        ),
        name="attend",
    )(lengths, image_tokens, text_tokens, image_weight, text_weight, gate_values)
    return store(outs)


def solution(mesh):
    in_specs = (
        P(None, ("grp", "blk"), None),
        P(None, ("grp", "blk"), None),
        P("grp"),
        P("grp", None),
        P("grp", None),
        P("grp", None, None),
    )
    out_specs = (P(("grp", "blk"), None), P(("grp", "blk"), None))
    return jax.shard_map(
        per_device, mesh=mesh, in_specs=in_specs, out_specs=out_specs, check_vma=False
    )
```

```python
import functools

import jax
import jax.numpy as jnp
from jax import lax
from jax.experimental import pallas as pl
from jax.experimental.pallas import tpu as pltpu
from jax.sharding import PartitionSpec as P

HEADS = 38
LANES = 128
MESH = pl.DeviceIdType.MESH


def remote(src, dst, send, recv, axis, peer):
    return pltpu.make_async_remote_copy(
        src_ref=src, dst_ref=dst, send_sem=send, recv_sem=recv,
        device_id={axis: peer}, device_id_type=MESH)


def row_parts(rows, parts, unit):
    base, extra = divmod(rows // unit, parts)
    sizes = [(base + (1 if j < extra else 0)) * unit for j in range(parts)]
    return [(sum(sizes[:j]), sizes[j]) for j in range(parts) if sizes[j]]


def column_tiles(width, tile):
    return [(at, min(tile, width - at)) for at in range(0, width, tile)]


class WeightGather:
    def __init__(self, group_count, shard, full, send, far, near):
        self.shard, self.full = shard, full
        self.send, self.far_sem, self.near_sem = send, far, near
        self.rows = shard.shape[0]
        self.unit = 16 if self.rows % 16 == 0 else 8
        self.bits = group_count.bit_length() - 1
        self.far = list(range(1, self.bits))
        self.parts = row_parts(self.rows, max(1, len(self.far)), self.unit)
        self.me = lax.axis_index("grp")

    def flip(self, mask):
        at = self.me
        for k in range(self.bits):
            if mask >> k & 1:
                at = at + (1 - 2 * ((self.me // (1 << k)) % 2)) * (1 << k)
        return at

    def order(self, j):
        return self.far[j:] + self.far[:j] if self.far else []

    def masks(self, level):
        return [m for m in range(0, 1 << self.bits, 2) if bin(m).count("1") == level]

    def cuts(self, j, mask):
        first, size = self.parts[j]
        if mask.bit_count() < len(self.far):
            return [(first, size)]
        head = size * 2 // 3 // self.unit * self.unit
        return [(first, head), (first + head, size - head)]

    def piece(self, mask, rows):
        return self.full.at[pl.ds(pl.multiple_of(self.flip(mask) * self.rows + rows[0], self.unit), rows[1]), :]

    def source(self, mask, rows):
        return self.shard.at[pl.ds(*rows), :] if mask == 0 else self.piece(mask, rows)

    def shards(self, count):
        return self.full.at[pl.ds(0, count * self.rows), :]

    def own(self):
        return pltpu.make_async_copy(
            self.shard, self.full.at[pl.ds(pl.multiple_of(self.me * self.rows, self.unit), self.rows), :],
            self.near_sem.at[0])

    def wait(self, count, sem):
        pltpu.make_async_copy(self.shards(count), self.shards(count), sem).wait()

    def near(self, mask, rows):
        if self.bits:
            remote(self.source(mask, rows), self.piece(mask, rows), self.send, self.near_sem.at[mask.bit_count()],
                   "grp", self.flip(1)).start()

    def advance(self, level):
        if level > 0:
            self.wait(len(self.masks(level)), self.far_sem.at[level])
        for mask in self.masks(level):
            for j in range(len(self.parts)):
                order = self.order(j)
                done = max([order.index(k) for k in order if mask >> k & 1], default=-1)
                for k in order[done + 1:]:
                    there = mask | 1 << k
                    for i, rows in enumerate(self.cuts(j, there)):
                        remote(self.source(mask, rows), self.piece(mask, rows), self.send,
                               self.far_sem.at[level + 1 + i], "grp", self.flip(1 << k)).start()
                self.near(mask, self.parts[j])
        if level == 0:
            self.own().start()

    def advance_last(self, i):
        level = len(self.far)
        if level == 0:
            return
        (mask,) = self.masks(level)
        ranges = [self.cuts(j, mask)[i] for j in range(len(self.parts))]
        ref = self.full.at[pl.ds(0, sum(size for _, size in ranges)), :]
        pltpu.make_async_copy(ref, ref, self.far_sem.at[level + i]).wait()
        for rows in ranges:
            self.near(mask, rows)

    def finish(self, level):
        if level <= len(self.far):
            self.wait((len(self.masks(level)) if self.bits else 0) + (level == 0), self.near_sem.at[level])

    def drain(self):
        far = 1 << len(self.far)
        if self.bits:
            self.wait(far - 1 + far, self.send)


def block_kernel(
    n, group_count, head_size,
    length_in, img, txt, image_shard, text_shard, gates_in, out_img, out_txt,
    length, gates,
    qkv, shared_kv, shared_q, attended, done, keys, first_values, second_values, valid, image_full, text_full,
    image_acc, text_acc,
    in_send, in_recv, out_send, out_recv, kv_send, kv_recv, shared_local, w_send, w_far, w_near, small_local,
):
    me = lax.axis_index("blk")
    image_rows, text_rows, width = img.shape[1], txt.shape[1], img.shape[2]
    span = image_rows + text_rows
    pairs = width // LANES
    base, extra = divmod(pairs, n)
    streams = ((img, 0, image_rows), (txt, image_rows, text_rows))

    weights = [
        WeightGather(group_count, shard, full, w_send.at[i], w_far.at[i], w_near.at[i])
        for i, (shard, full) in enumerate(((image_shard, image_full), (text_shard, text_full)))
    ]

    length_copy = pltpu.make_async_copy(length_in, length, small_local.at[0])
    gates_copy = pltpu.make_async_copy(gates_in, gates, small_local.at[1])
    length_copy.start()
    gates_copy.start()

    barrier = pltpu.get_barrier_semaphore()
    for d in range(1, n):
        pl.semaphore_signal(barrier, inc=1, device_id={"blk": lax.rem(me + d, n)}, device_id_type=MESH)
    for k in range(weights[0].bits):
        pl.semaphore_signal(barrier, inc=1, device_id={"grp": weights[0].flip(1 << k)}, device_id_type=MESH)
    pl.semaphore_wait(barrier, n - 1 + weights[0].bits)

    def columns(b, p):
        return pl.ds(pl.multiple_of((b * base + p) * LANES, LANES), LANES)

    def rows_of(b, first, count):
        return pl.ds(pl.multiple_of(b * span + first, 16), count)

    def in_copies(p, dest):
        return [
            remote(src.at[:, :, columns(dest, p)], qkv.at[p, :, rows_of(me, first, count), :],
                   in_send, in_recv.at[p], "blk", dest)
            for src, first, count in streams
        ]

    def own_copies(p):
        return [
            pltpu.make_async_copy(
                src.at[:, :, columns(me, p)], qkv.at[p, :, rows_of(me, first, count), :], in_recv.at[p])
            for src, first, count in streams
        ]

    middle = n // 2
    split = n % 2 == 0

    def out_copy(p, dest):
        across = jnp.where((me < middle) == (dest < middle), 0, 1) if split else 0
        return remote(done.at[p, dest], attended.at[me * base + p], out_send, out_recv.at[p, across], "blk", dest)

    def own_out(p):
        return pltpu.make_async_copy(done.at[p, me], attended.at[me * base + p], out_recv.at[p, 0])

    def wait_bytes(ref, sem):
        pltpu.make_async_copy(ref, ref, sem).wait()

    shared_cols = pl.ds(n * base * LANES, extra * LANES)

    halves = (range(middle), range(middle, n))
    doors = (middle - 1, middle)

    def kv_direct(dest, across):
        return [
            remote(src.at[pl.ds(1, 2), :, shared_cols], shared_kv.at[:, rows_of(me, first, count), :],
                   kv_send, kv_recv.at[across], "blk", dest)
            for src, first, count in streams
        ]

    def kv_onward(owner, dest):
        block = shared_kv.at[:, rows_of(owner, 0, span), :]
        return remote(block, block, kv_send, kv_recv.at[1], "blk", dest)

    def kv_wait(blocks, sem):
        if blocks:
            wait_bytes(shared_kv.at[:, pl.ds(0, blocks * span), :], sem)

    def shared_own():
        copies = []
        for src, first, count in streams:
            copies.append(pltpu.make_async_copy(
                src.at[pl.ds(1, 2), :, shared_cols], shared_kv.at[:, rows_of(me, first, count), :], kv_recv.at[0]))
            copies.append(pltpu.make_async_copy(
                src.at[0, :, shared_cols], shared_q.at[pl.ds(first, count), :], shared_local))
        return copies

    def each_half(act):
        for side in range(2):
            if len(halves[side]):
                @pl.when((me < middle) if side == 0 else (me >= middle))
                def _():
                    act(side)

    def start_shared():
        def act(side):
            if len(halves[1 - side]):
                for copy in kv_direct(doors[1 - side], 1):
                    copy.start()
            for dest in halves[side]:
                @pl.when(dest != me)
                def _():
                    for copy in kv_direct(dest, 0):
                        copy.start()

        each_half(act)
        for copy in shared_own():
            copy.start()

    def pass_shared():
        def act(side):
            @pl.when(me == doors[side])
            def _():
                kv_wait(len(halves[1 - side]), kv_recv.at[1])
                for owner in halves[1 - side]:
                    for dest in halves[side]:
                        if dest != doors[side]:
                            kv_onward(owner, dest).start()

        each_half(act)

    def finish_shared():
        wait_bytes(shared_q, shared_local)

        def act(side):
            kv_wait(len(halves[side]), kv_recv.at[0])

            @pl.when(me != doors[side])
            def _():
                kv_wait(len(halves[1 - side]), kv_recv.at[1])

        each_half(act)

    def drain_shared():
        def act(side):
            own, other = len(halves[side]), len(halves[1 - side])
            kv_wait(own - 1 + (other > 0), kv_send)

            @pl.when(me == doors[side])
            def _():
                for _ in range(own - 1):
                    kv_wait(other, kv_send)

        each_half(act)

    order = sorted(range(1, n), key=lambda d: abs(d - n / 2))

    def send_in(p):
        for d in order:
            for copy in in_copies(p, lax.rem(me + d, n)):
                copy.start()
        for copy in own_copies(p):
            copy.start()

    first_half = lax.broadcasted_iota(jnp.int32, (span, LANES), 1) < head_size

    def prepare(block_keys, block_values):
        half = lax.broadcasted_iota(jnp.int32, (n * span, LANES), 1) < head_size
        ones = jnp.ones((n * span, LANES), jnp.bfloat16)
        usable = valid[...]
        k = block_keys()
        keys[...] = jnp.where(usable > 0.5, k, jnp.broadcast_to(k[0:1], k.shape))
        v = block_values()
        first_values[...] = jnp.where(half, v, ones) * usable
        second_values[...] = jnp.where(half, ones, v) * usable

    def attend_rows(queries):
        queries = queries * jnp.asarray(head_size ** (-0.5), jnp.bfloat16)
        zeros = jnp.zeros_like(queries)
        parts = []
        for own, values in ((jnp.where(first_half, queries, zeros), first_values),
                            (jnp.where(first_half, zeros, queries), second_values)):
            scores = lax.dot_general(own, keys[...], (((1,), (1,)), ((), ())), preferred_element_type=jnp.float32)
            probs = jnp.exp(scores - jnp.max(scores, axis=1, keepdims=True)).astype(jnp.bfloat16)
            parts.append(jnp.dot(probs, values[...], preferred_element_type=jnp.float32))
        summed = jnp.where(first_half, parts[0], parts[1])
        totals = pltpu.roll(jnp.where(first_half, parts[1], parts[0]), head_size, axis=1)
        return (summed / totals).astype(jnp.bfloat16)

    def attend_pair(p):
        wait_bytes(qkv.at[p], in_recv.at[p])
        prepare(lambda: qkv[p, 1], lambda: qkv[p, 2])

        def one_block(j, _):
            dest = lax.rem(me + n // 2 + j, n)
            done[p, dest] = attend_rows(qkv[p, 0, rows_of(dest, 0, span), :])

            @pl.when(dest != me)
            def _():
                out_copy(p, dest).start()

            return 0

        lax.fori_loop(0, n, one_block, 0)
        own_out(p).start()

    def attend_shared():
        finish_shared()
        for e in range(extra):
            cols = pl.ds(e * LANES, LANES)
            prepare(lambda: shared_kv[0, :, cols], lambda: shared_kv[1, :, cols])
            attended[n * base + e] = attend_rows(shared_q[:, cols])

    def project(acc, full, rows, chosen, start, finish):
        left = jnp.concatenate([attended[c, rows, :] for c in chosen], axis=1)
        for at, size in column_tiles(width, 256):
            right = jnp.concatenate([full[pl.ds(pl.multiple_of(c * LANES, LANES), LANES), pl.ds(at, size)] for c in chosen], axis=0)
            part = jnp.dot(left, right, preferred_element_type=jnp.float32)
            if not start:
                part = part + acc[:, pl.ds(at, size)]
            if finish is None:
                acc[:, pl.ds(at, size)] = part
            else:
                out, gate = finish
                out[:, pl.ds(at, size)] = (part * gates[0, pl.ds(gate, 1), pl.ds(at, size)]).astype(jnp.bfloat16)

    def text_step(c):
        part = jnp.dot(attended[c, text_span, :], text_full[pl.ds(pl.multiple_of(c * LANES, LANES), LANES), :],
                       preferred_element_type=jnp.float32)
        text_acc[...] += part

    def early_text(first, stride, count):
        def step(i, _):
            c = first + stride * i

            @pl.when(lax.rem(c - late_first + pairs, pairs) >= late_pairs)
            def _():
                text_step(c)

            return 0

        lax.fori_loop(0, count, step, 0)

    late_rows = 2 * weights[1].rows if weights[1].bits else weights[1].rows
    late_pairs = min(pairs, -(-late_rows // LANES) + 1)
    late_first = weights[1].flip(sum(1 << k for k in weights[1].far)) // 2 * late_rows // LANES

    text_span = pl.ds(image_rows, text_rows)
    image_span = pl.ds(0, image_rows)

    if extra:
        start_shared()
    send_in(0)
    weights[0].advance(0)
    for p in range(1, base):
        send_in(p)
    weights[1].advance(0)

    length_copy.wait()
    for b in range(n):
        at = lax.broadcasted_iota(jnp.int32, (span, LANES), 0)
        usable = (at >= image_rows) | (b * image_rows + at < length[0])
        valid[pl.ds(b * span, span), :] = jnp.where(usable, 1.0, 0.0).astype(jnp.bfloat16)

    far_levels = len(weights[0].far)

    def advance(i, level):
        if level < far_levels:
            weights[i].advance(level)

    if extra:
        pass_shared()
    for p in range(base):
        if p == base - 1:
            if extra:
                attend_shared()
            for level in range(1 if base == 1 else 2, far_levels):
                weights[0].advance(level)
            for i in range(2):
                weights[0].advance_last(i)
        attend_pair(p)
        if p == 0 and base > 1:
            advance(0, 1)
        if p == min(1, base - 1):
            advance(1, 1)
    for level in range(far_levels + 1):
        weights[0].finish(level)
    gates_copy.wait()

    def wait_out(p, across):
        wait_bytes(attended.at[pl.ds(0, n // 2 if split else n)], out_recv.at[p, across])

    for level in range(2, far_levels):
        weights[1].advance(level)
    for level in range(far_levels):
        weights[1].finish(level)
    text_acc[...] = jnp.zeros_like(text_acc)
    started = bool(extra)
    if extra:
        project(image_acc, image_full, image_span, [n * base + e for e in range(extra)], True, None)
        early_text(n * base, 1, extra)
    if base < 3:
        weights[1].advance_last(0)
    near_first = jnp.where(me < middle, 0, middle) if split else 0
    for p in range(base):
        last = p == base - 1
        if p >= base - 2 and split:
            groups = [(near_first, n // 2, 0), (middle - near_first, n // 2, 1)]
        else:
            groups = [(0, n, 0)]
        for first, count, across in groups:
            wait_out(p, across)
            if split and len(groups) == 1:
                wait_out(p, 1)
            if p == max(0, base - 2) and across == len(groups) - 1:
                weights[1].advance_last(1)
            ends = last and across == len(groups) - 1
            project(image_acc, image_full, image_span, [(first + b) * base + p for b in range(count)], not started,
                    (out_img, 0) if ends else None)
            started = True
            early_text(first * base + p, base, count)
        if p == base - 3:
            weights[1].advance_last(0)
    weights[1].finish(far_levels)
    for i in range(late_pairs):
        text_step(lax.rem(late_first + i, pairs))
    out_txt[...] = (text_acc[...] * gates[0, 1:2, :]).astype(jnp.bfloat16)

    wait_bytes(qkv.at[:, :, pl.ds(0, (n - 1) * span), :], in_send)
    for _ in range(base):
        wait_bytes(attended.at[pl.ds(0, n - 1)], out_send)
    if extra:
        drain_shared()
    for weight in weights:
        weight.drain()


def store_kernel(image_in, text_in, image_out, text_out, sems):
    copies = [pltpu.make_async_copy(image_in, image_out, sems.at[0]), pltpu.make_async_copy(text_in, text_out, sems.at[1])]
    for copy in copies:
        copy.start()
    for copy in copies:
        copy.wait()


def store(outs):
    return pl.pallas_call(
        store_kernel,
        out_shape=tuple(jax.ShapeDtypeStruct(x.shape, x.dtype) for x in outs),
        in_specs=[pl.BlockSpec(memory_space=pl.ANY)] * 2,
        out_specs=(pl.BlockSpec(memory_space=pltpu.HBM),) * 2,
        scratch_shapes=[pltpu.SemaphoreType.DMA((2,))],
        name="store",
    )(*[pltpu.with_memory_space_constraint(x, pltpu.VMEM) for x in outs])


def per_device(image_tokens, text_tokens, lengths, image_weight, text_weight, gate_values):
    image_rows, text_rows, width = image_tokens.shape[1], text_tokens.shape[1], image_tokens.shape[2]
    n, group_count = lax.axis_size("blk"), lax.axis_size("grp")
    span = image_rows + text_rows
    pairs = width // LANES
    base, extra = divmod(pairs, n)
    bits = group_count.bit_length() - 1
    levels = max(1, bits)
    dma = pltpu.SemaphoreType.DMA
    bf16, f32 = jnp.bfloat16, jnp.float32
    any_space = pl.BlockSpec(memory_space=pltpu.HBM)
    vmem = pl.BlockSpec(memory_space=pltpu.VMEM)
    wide = max(1, extra) * LANES
    outs = pl.pallas_call(
        functools.partial(block_kernel, n, group_count, width // HEADS),
        out_shape=(
            pltpu.VMEM((image_rows, width), bf16),
            pltpu.VMEM((text_rows, width), bf16),
        ),
        in_specs=[any_space] * 6,
        out_specs=(vmem, vmem),
        scratch_shapes=[
            pltpu.SMEM((1,), jnp.int32),
            pltpu.VMEM((1, 2, width), f32),
            pltpu.VMEM((base, 3, n * span, LANES), bf16),
            pltpu.VMEM((2, n * span, wide), bf16),
            pltpu.VMEM((span, wide), bf16),
            pltpu.VMEM((pairs, span, LANES), bf16),
            pltpu.VMEM((base, n, span, LANES), bf16),
            pltpu.VMEM((n * span, LANES), bf16),
            pltpu.VMEM((n * span, LANES), bf16),
            pltpu.VMEM((n * span, LANES), bf16),
            pltpu.VMEM((n * span, LANES), bf16),
            pltpu.VMEM((width, width), bf16),
            pltpu.VMEM((width, width), bf16),
            pltpu.VMEM((image_rows, width), f32),
            pltpu.VMEM((text_rows, width), f32),
            dma, dma((base,)), dma, dma((base, 2)), dma, dma((2,)), dma,
            dma((2,)), dma((2, levels + 1)), dma((2, levels)), dma((2,)),
        ],
        compiler_params=pltpu.CompilerParams(
            collective_id=0, has_side_effects=True, vmem_limit_bytes=60 * 1024 * 1024
        ),
        name="attend",
    )(lengths, image_tokens, text_tokens, image_weight, text_weight, gate_values)
    return store(outs)


def solution(mesh):
    in_specs = (
        P(None, ("grp", "blk"), None),
        P(None, ("grp", "blk"), None),
        P("grp"),
        P("grp", None),
        P("grp", None),
        P("grp", None, None),
    )
    out_specs = (P(("grp", "blk"), None), P(("grp", "blk"), None))
    return jax.shard_map(
        per_device, mesh=mesh, in_specs=in_specs, out_specs=out_specs, check_vma=False
    )
```

```python
import functools

import jax
import jax.numpy as jnp
from jax import lax
from jax.experimental import pallas as pl
from jax.experimental.pallas import tpu as pltpu
from jax.sharding import PartitionSpec as P

HEADS = 38
LANES = 128
MESH = pl.DeviceIdType.MESH


def remote(src, dst, send, recv, axis, peer):
    return pltpu.make_async_remote_copy(
        src_ref=src, dst_ref=dst, send_sem=send, recv_sem=recv,
        device_id={axis: peer}, device_id_type=MESH)


def row_parts(rows, parts, unit):
    base, extra = divmod(rows // unit, parts)
    sizes = [(base + (1 if j < extra else 0)) * unit for j in range(parts)]
    return [(sum(sizes[:j]), sizes[j]) for j in range(parts) if sizes[j]]


def column_tiles(width, tile):
    return [(at, min(tile, width - at)) for at in range(0, width, tile)]


def late_rows(group_count, pairs):
    rows = pairs * LANES // group_count
    me, at = lax.axis_index("grp"), lax.axis_index("grp")
    bits = group_count.bit_length() - 1
    for k in range(1, bits):
        at = at + (1 - 2 * ((me // (1 << k)) % 2)) * (1 << k)
    span = 2 * rows if bits else rows
    return at // 2 * span // LANES, min(pairs, -(-span // LANES) + 1)


class WeightGather:
    def __init__(self, group_count, shard, full, send, far, near):
        self.shard, self.full = shard, full
        self.send, self.far_sem, self.near_sem = send, far, near
        self.rows = shard.shape[0]
        self.unit = 16 if self.rows % 16 == 0 else 8
        self.bits = group_count.bit_length() - 1
        self.far = list(range(1, self.bits))
        self.parts = row_parts(self.rows, max(1, len(self.far)), self.unit)
        self.me = lax.axis_index("grp")

    def flip(self, mask):
        at = self.me
        for k in range(self.bits):
            if mask >> k & 1:
                at = at + (1 - 2 * ((self.me // (1 << k)) % 2)) * (1 << k)
        return at

    def order(self, j):
        return self.far[j:] + self.far[:j] if self.far else []

    def masks(self, level):
        return [m for m in range(0, 1 << self.bits, 2) if bin(m).count("1") == level]

    def cuts(self, j, mask):
        first, size = self.parts[j]
        if mask.bit_count() < len(self.far):
            return [(first, size)]
        head = size * 2 // 3 // self.unit * self.unit
        return [(first, head), (first + head, size - head)]

    def piece(self, mask, rows):
        return self.full.at[pl.ds(pl.multiple_of(self.flip(mask) * self.rows + rows[0], self.unit), rows[1]), :]

    def source(self, mask, rows):
        return self.shard.at[pl.ds(*rows), :] if mask == 0 else self.piece(mask, rows)

    def shards(self, count):
        return self.full.at[pl.ds(0, count * self.rows), :]

    def own(self):
        return pltpu.make_async_copy(
            self.shard, self.full.at[pl.ds(pl.multiple_of(self.me * self.rows, self.unit), self.rows), :],
            self.near_sem.at[0])

    def wait(self, count, sem):
        pltpu.make_async_copy(self.shards(count), self.shards(count), sem).wait()

    def near(self, mask, rows):
        if self.bits:
            remote(self.source(mask, rows), self.piece(mask, rows), self.send, self.near_sem.at[mask.bit_count()],
                   "grp", self.flip(1)).start()

    def advance(self, level):
        if level > 0:
            self.wait(len(self.masks(level)), self.far_sem.at[level])
        for mask in self.masks(level):
            for j in range(len(self.parts)):
                order = self.order(j)
                done = max([order.index(k) for k in order if mask >> k & 1], default=-1)
                for k in order[done + 1:]:
                    there = mask | 1 << k
                    for i, rows in enumerate(self.cuts(j, there)):
                        remote(self.source(mask, rows), self.piece(mask, rows), self.send,
                               self.far_sem.at[level + 1 + i], "grp", self.flip(1 << k)).start()
                self.near(mask, self.parts[j])
        if level == 0:
            self.own().start()

    def advance_last(self, i):
        level = len(self.far)
        if level == 0:
            return
        (mask,) = self.masks(level)
        ranges = [self.cuts(j, mask)[i] for j in range(len(self.parts))]
        ref = self.full.at[pl.ds(0, sum(size for _, size in ranges)), :]
        pltpu.make_async_copy(ref, ref, self.far_sem.at[level + i]).wait()
        for rows in ranges:
            self.near(mask, rows)

    def finish(self, level):
        if level <= len(self.far):
            self.wait((len(self.masks(level)) if self.bits else 0) + (level == 0), self.near_sem.at[level])

    def drain(self):
        far = 1 << len(self.far)
        if self.bits:
            self.wait(far - 1 + far, self.send)


def block_kernel(
    n, group_count, head_size,
    length_in, img, txt, image_shard, text_shard, gates_in,
    out_img, text_full, attended, text_acc, gates, length,
    qkv, shared_kv, shared_q, done, keys, first_values, second_values, valid, image_full, image_acc,
    in_send, in_recv, out_send, out_recv, kv_send, kv_recv, shared_local, w_send, w_far, w_near, small_local,
):
    me = lax.axis_index("blk")
    image_rows, text_rows, width = img.shape[1], txt.shape[1], img.shape[2]
    span = image_rows + text_rows
    pairs = width // LANES
    base, extra = divmod(pairs, n)
    streams = ((img, 0, image_rows), (txt, image_rows, text_rows))

    weights = [
        WeightGather(group_count, shard, full, w_send.at[i], w_far.at[i], w_near.at[i])
        for i, (shard, full) in enumerate(((image_shard, image_full), (text_shard, text_full)))
    ]

    length_copy = pltpu.make_async_copy(length_in, length, small_local.at[0])
    gates_copy = pltpu.make_async_copy(gates_in, gates, small_local.at[1])
    length_copy.start()
    gates_copy.start()

    barrier = pltpu.get_barrier_semaphore()
    for d in range(1, n):
        pl.semaphore_signal(barrier, inc=1, device_id={"blk": lax.rem(me + d, n)}, device_id_type=MESH)
    for k in range(weights[0].bits):
        pl.semaphore_signal(barrier, inc=1, device_id={"grp": weights[0].flip(1 << k)}, device_id_type=MESH)
    pl.semaphore_wait(barrier, n - 1 + weights[0].bits)

    def columns(b, p):
        return pl.ds(pl.multiple_of((b * base + p) * LANES, LANES), LANES)

    def rows_of(b, first, count):
        return pl.ds(pl.multiple_of(b * span + first, 16), count)

    def in_copies(p, dest):
        return [
            remote(src.at[:, :, columns(dest, p)], qkv.at[p, :, rows_of(me, first, count), :],
                   in_send, in_recv.at[p], "blk", dest)
            for src, first, count in streams
        ]

    def own_copies(p):
        return [
            pltpu.make_async_copy(
                src.at[:, :, columns(me, p)], qkv.at[p, :, rows_of(me, first, count), :], in_recv.at[p])
            for src, first, count in streams
        ]

    middle = n // 2
    split = n % 2 == 0

    def out_copy(p, dest):
        across = jnp.where((me < middle) == (dest < middle), 0, 1) if split else 0
        return remote(done.at[p, dest], attended.at[me * base + p], out_send, out_recv.at[p, across], "blk", dest)

    def own_out(p):
        return pltpu.make_async_copy(done.at[p, me], attended.at[me * base + p], out_recv.at[p, 0])

    def wait_bytes(ref, sem):
        pltpu.make_async_copy(ref, ref, sem).wait()

    shared_cols = pl.ds(n * base * LANES, extra * LANES)

    halves = (range(middle), range(middle, n))
    doors = (middle - 1, middle)

    def kv_direct(dest, across):
        return [
            remote(src.at[pl.ds(1, 2), :, shared_cols], shared_kv.at[:, rows_of(me, first, count), :],
                   kv_send, kv_recv.at[across], "blk", dest)
            for src, first, count in streams
        ]

    def kv_onward(owner, dest):
        block = shared_kv.at[:, rows_of(owner, 0, span), :]
        return remote(block, block, kv_send, kv_recv.at[1], "blk", dest)

    def kv_wait(blocks, sem):
        if blocks:
            wait_bytes(shared_kv.at[:, pl.ds(0, blocks * span), :], sem)

    def shared_own():
        copies = []
        for src, first, count in streams:
            copies.append(pltpu.make_async_copy(
                src.at[pl.ds(1, 2), :, shared_cols], shared_kv.at[:, rows_of(me, first, count), :], kv_recv.at[0]))
            copies.append(pltpu.make_async_copy(
                src.at[0, :, shared_cols], shared_q.at[pl.ds(first, count), :], shared_local))
        return copies

    def each_half(act):
        for side in range(2):
            if len(halves[side]):
                @pl.when((me < middle) if side == 0 else (me >= middle))
                def _():
                    act(side)

    def start_shared():
        def act(side):
            if len(halves[1 - side]):
                for copy in kv_direct(doors[1 - side], 1):
                    copy.start()
            for dest in halves[side]:
                @pl.when(dest != me)
                def _():
                    for copy in kv_direct(dest, 0):
                        copy.start()

        each_half(act)
        for copy in shared_own():
            copy.start()

    def pass_shared():
        def act(side):
            @pl.when(me == doors[side])
            def _():
                kv_wait(len(halves[1 - side]), kv_recv.at[1])
                for owner in halves[1 - side]:
                    for dest in halves[side]:
                        if dest != doors[side]:
                            kv_onward(owner, dest).start()

        each_half(act)

    def finish_shared():
        wait_bytes(shared_q, shared_local)

        def act(side):
            kv_wait(len(halves[side]), kv_recv.at[0])

            @pl.when(me != doors[side])
            def _():
                kv_wait(len(halves[1 - side]), kv_recv.at[1])

        each_half(act)

    def drain_shared():
        def act(side):
            own, other = len(halves[side]), len(halves[1 - side])
            kv_wait(own - 1 + (other > 0), kv_send)

            @pl.when(me == doors[side])
            def _():
                for _ in range(own - 1):
                    kv_wait(other, kv_send)

        each_half(act)

    order = sorted(range(1, n), key=lambda d: abs(d - n / 2))

    def send_in(p):
        for d in order:
            for copy in in_copies(p, lax.rem(me + d, n)):
                copy.start()
        for copy in own_copies(p):
            copy.start()

    first_half = lax.broadcasted_iota(jnp.int32, (span, LANES), 1) < head_size

    def prepare(block_keys, block_values):
        half = lax.broadcasted_iota(jnp.int32, (n * span, LANES), 1) < head_size
        ones = jnp.ones((n * span, LANES), jnp.bfloat16)
        usable = valid[...]
        k = block_keys()
        keys[...] = jnp.where(usable > 0.5, k, jnp.broadcast_to(k[0:1], k.shape))
        v = block_values()
        first_values[...] = jnp.where(half, v, ones) * usable
        second_values[...] = jnp.where(half, ones, v) * usable

    def attend_rows(queries):
        queries = queries * jnp.asarray(head_size ** (-0.5), jnp.bfloat16)
        zeros = jnp.zeros_like(queries)
        parts = []
        for own, values in ((jnp.where(first_half, queries, zeros), first_values),
                            (jnp.where(first_half, zeros, queries), second_values)):
            scores = lax.dot_general(own, keys[...], (((1,), (1,)), ((), ())), preferred_element_type=jnp.float32)
            probs = jnp.exp(scores - jnp.max(scores, axis=1, keepdims=True)).astype(jnp.bfloat16)
            parts.append(jnp.dot(probs, values[...], preferred_element_type=jnp.float32))
        summed = jnp.where(first_half, parts[0], parts[1])
        totals = pltpu.roll(jnp.where(first_half, parts[1], parts[0]), head_size, axis=1)
        return (summed / totals).astype(jnp.bfloat16)

    def attend_pair(p):
        wait_bytes(qkv.at[p], in_recv.at[p])
        prepare(lambda: qkv[p, 1], lambda: qkv[p, 2])

        def one_block(j, _):
            dest = lax.rem(me + n // 2 + j, n)
            done[p, dest] = attend_rows(qkv[p, 0, rows_of(dest, 0, span), :])

            @pl.when(dest != me)
            def _():
                out_copy(p, dest).start()

            return 0

        lax.fori_loop(0, n, one_block, 0)
        own_out(p).start()

    def attend_shared():
        finish_shared()
        for e in range(extra):
            cols = pl.ds(e * LANES, LANES)
            prepare(lambda: shared_kv[0, :, cols], lambda: shared_kv[1, :, cols])
            attended[n * base + e] = attend_rows(shared_q[:, cols])

    def project(acc, full, rows, chosen, start, finish):
        left = jnp.concatenate([attended[c, rows, :] for c in chosen], axis=1)
        for at, size in column_tiles(width, 256):
            right = jnp.concatenate([full[pl.ds(pl.multiple_of(c * LANES, LANES), LANES), pl.ds(at, size)] for c in chosen], axis=0)
            part = jnp.dot(left, right, preferred_element_type=jnp.float32)
            if not start:
                part = part + acc[:, pl.ds(at, size)]
            if finish is None:
                acc[:, pl.ds(at, size)] = part
            else:
                out, gate = finish
                out[:, pl.ds(at, size)] = (part * gates[0, pl.ds(gate, 1), pl.ds(at, size)]).astype(jnp.bfloat16)

    def text_step(c):
        part = jnp.dot(attended[c, text_span, :], text_full[pl.ds(pl.multiple_of(c * LANES, LANES), LANES), :],
                       preferred_element_type=jnp.float32)
        text_acc[...] += part

    def early_text(first, stride, count):
        def step(i, _):
            c = first + stride * i

            @pl.when(lax.rem(c - late_first + pairs, pairs) >= late_pairs)
            def _():
                text_step(c)

            return 0

        lax.fori_loop(0, count, step, 0)

    late_first, late_pairs = late_rows(group_count, pairs)

    text_span = pl.ds(image_rows, text_rows)
    image_span = pl.ds(0, image_rows)

    if extra:
        start_shared()
    send_in(0)
    weights[0].advance(0)
    for p in range(1, base):
        send_in(p)
    weights[1].advance(0)

    length_copy.wait()
    for b in range(n):
        at = lax.broadcasted_iota(jnp.int32, (span, LANES), 0)
        usable = (at >= image_rows) | (b * image_rows + at < length[0])
        valid[pl.ds(b * span, span), :] = jnp.where(usable, 1.0, 0.0).astype(jnp.bfloat16)

    far_levels = len(weights[0].far)

    def advance(i, level):
        if level < far_levels:
            weights[i].advance(level)

    if extra:
        pass_shared()
    for p in range(base):
        if p == base - 1:
            if extra:
                attend_shared()
            for level in range(1 if base == 1 else 2, far_levels):
                weights[0].advance(level)
            for i in range(2):
                weights[0].advance_last(i)
        attend_pair(p)
        if p == 0 and base > 1:
            advance(0, 1)
        if p == min(1, base - 1):
            advance(1, 1)
    for level in range(far_levels + 1):
        weights[0].finish(level)
    gates_copy.wait()

    def wait_out(p, across):
        wait_bytes(attended.at[pl.ds(0, n // 2 if split else n)], out_recv.at[p, across])

    for level in range(2, far_levels):
        weights[1].advance(level)
    for level in range(far_levels):
        weights[1].finish(level)
    text_acc[...] = jnp.zeros_like(text_acc)
    started = bool(extra)
    if extra:
        project(image_acc, image_full, image_span, [n * base + e for e in range(extra)], True, None)
        early_text(n * base, 1, extra)
    if base < 3:
        weights[1].advance_last(0)
    near_first = jnp.where(me < middle, 0, middle) if split else 0
    for p in range(base):
        last = p == base - 1
        if p >= base - 2 and split:
            groups = [(near_first, n // 2, 0), (middle - near_first, n // 2, 1)]
        else:
            groups = [(0, n, 0)]
        for first, count, across in groups:
            wait_out(p, across)
            if split and len(groups) == 1:
                wait_out(p, 1)
            if p == max(0, base - 2) and across == len(groups) - 1:
                weights[1].advance_last(1)
            ends = last and across == len(groups) - 1
            project(image_acc, image_full, image_span, [(first + b) * base + p for b in range(count)], not started,
                    (out_img, 0) if ends else None)
            started = True
            if not ends:
                early_text(first * base + p, base, count)
        if p == base - 3:
            weights[1].advance_last(0)
    weights[1].finish(far_levels)

    wait_bytes(qkv.at[:, :, pl.ds(0, (n - 1) * span), :], in_send)
    for _ in range(base):
        wait_bytes(attended.at[pl.ds(0, n - 1)], out_send)
    if extra:
        drain_shared()
    for weight in weights:
        weight.drain()


def store_kernel(n, group_count, image_in, text_full, attended, text_acc, gates, image_out, text_out, text_done, sems):
    image_copy = pltpu.make_async_copy(image_in, image_out, sems.at[0])
    image_copy.start()
    pairs, text_rows = attended.shape[0], text_done.shape[0]
    image_rows = attended.shape[1] - text_rows
    base = pairs // n
    late_first, late_pairs = late_rows(group_count, pairs)
    left, chosen = [], []
    for i in range(late_pairs):
        c = lax.rem(late_first + i, pairs)
        left.append(attended[c, pl.ds(image_rows, text_rows), :])
        chosen.append(c)
    middle, count = n // 2, n // 2 if n % 2 == 0 else n
    first = jnp.where(lax.axis_index("blk") < middle, middle, 0) if n % 2 == 0 else 0
    for b in range(count):
        c = (first + b) * base + base - 1
        rows = attended[c, pl.ds(image_rows, text_rows), :]
        left.append(jnp.where(lax.rem(c - late_first + pairs, pairs) >= late_pairs, rows, jnp.zeros_like(rows)))
        chosen.append(c)
    left = jnp.concatenate(left, axis=1)
    for at, size in column_tiles(text_done.shape[1], 256):
        cols = pl.ds(at, size)
        right = jnp.concatenate(
            [text_full[pl.ds(pl.multiple_of(c * LANES, LANES), LANES), cols] for c in chosen], axis=0)
        total = text_acc[:, cols] + jnp.dot(left, right, preferred_element_type=jnp.float32)
        text_done[:, cols] = (total * gates[0, 1:2, cols]).astype(jnp.bfloat16)
    text_copy = pltpu.make_async_copy(text_done, text_out, sems.at[1])
    text_copy.start()
    text_copy.wait()
    image_copy.wait()


def store(n, group_count, outs):
    image, text_full, attended, text_acc, gates = [pltpu.with_memory_space_constraint(x, pltpu.VMEM) for x in outs]
    text = jax.ShapeDtypeStruct(text_acc.shape, jnp.bfloat16)
    vmem, hbm = pl.BlockSpec(memory_space=pltpu.VMEM), pl.BlockSpec(memory_space=pltpu.HBM)
    return pl.pallas_call(
        functools.partial(store_kernel, n, group_count),
        out_shape=(jax.ShapeDtypeStruct(image.shape, image.dtype), text),
        in_specs=[vmem] * 5,
        out_specs=(hbm, hbm),
        scratch_shapes=[
            pltpu.VMEM(text.shape, text.dtype), pltpu.SemaphoreType.DMA((2,)),
        ],
        compiler_params=pltpu.CompilerParams(vmem_limit_bytes=8 * 1024 * 1024),
        name="store",
    )(image, text_full, attended, text_acc, gates)


def per_device(image_tokens, text_tokens, lengths, image_weight, text_weight, gate_values):
    image_rows, text_rows, width = image_tokens.shape[1], text_tokens.shape[1], image_tokens.shape[2]
    n, group_count = lax.axis_size("blk"), lax.axis_size("grp")
    span = image_rows + text_rows
    pairs = width // LANES
    base, extra = divmod(pairs, n)
    bits = group_count.bit_length() - 1
    levels = max(1, bits)
    dma = pltpu.SemaphoreType.DMA
    bf16, f32 = jnp.bfloat16, jnp.float32
    any_space = pl.BlockSpec(memory_space=pltpu.HBM)
    vmem = pl.BlockSpec(memory_space=pltpu.VMEM)
    wide = max(1, extra) * LANES
    outs = pl.pallas_call(
        functools.partial(block_kernel, n, group_count, width // HEADS),
        out_shape=(
            pltpu.VMEM((image_rows, width), bf16),
            pltpu.VMEM((width, width), bf16),
            pltpu.VMEM((pairs, span, LANES), bf16),
            pltpu.VMEM((text_rows, width), f32),
            pltpu.VMEM((1, 2, width), f32),
        ),
        in_specs=[any_space] * 6,
        out_specs=(vmem,) * 5,
        scratch_shapes=[
            pltpu.SMEM((1,), jnp.int32),
            pltpu.VMEM((base, 3, n * span, LANES), bf16),
            pltpu.VMEM((2, n * span, wide), bf16),
            pltpu.VMEM((span, wide), bf16),
            pltpu.VMEM((base, n, span, LANES), bf16),
            pltpu.VMEM((n * span, LANES), bf16),
            pltpu.VMEM((n * span, LANES), bf16),
            pltpu.VMEM((n * span, LANES), bf16),
            pltpu.VMEM((n * span, LANES), bf16),
            pltpu.VMEM((width, width), bf16),
            pltpu.VMEM((image_rows, width), f32),
            dma, dma((base,)), dma, dma((base, 2)), dma, dma((2,)), dma,
            dma((2,)), dma((2, levels + 1)), dma((2, levels)), dma((2,)),
        ],
        compiler_params=pltpu.CompilerParams(
            collective_id=0, has_side_effects=True, vmem_limit_bytes=47 * 1024 * 1024
        ),
        name="attend",
    )(lengths, image_tokens, text_tokens, image_weight, text_weight, gate_values)
    return store(n, group_count, outs)


def solution(mesh):
    in_specs = (
        P(None, ("grp", "blk"), None),
        P(None, ("grp", "blk"), None),
        P("grp"),
        P("grp", None),
        P("grp", None),
        P("grp", None, None),
    )
    out_specs = (P(("grp", "blk"), None), P(("grp", "blk"), None))
    return jax.shard_map(
        per_device, mesh=mesh, in_specs=in_specs, out_specs=out_specs, check_vma=False
    )
```

```python
import functools

import jax
import jax.numpy as jnp
from jax import lax
from jax.experimental import pallas as pl
from jax.experimental.pallas import tpu as pltpu
from jax.sharding import PartitionSpec as P

HEADS = 38
LANES = 128
MESH = pl.DeviceIdType.MESH


def remote(src, dst, send, recv, axis, peer):
    return pltpu.make_async_remote_copy(
        src_ref=src, dst_ref=dst, send_sem=send, recv_sem=recv,
        device_id={axis: peer}, device_id_type=MESH)


def row_parts(rows, parts, unit):
    base, extra = divmod(rows // unit, parts)
    sizes = [(base + (1 if j < extra else 0)) * unit for j in range(parts)]
    return [(sum(sizes[:j]), sizes[j]) for j in range(parts) if sizes[j]]


def column_tiles(width, tile):
    return [(at, min(tile, width - at)) for at in range(0, width, tile)]


def late_rows(group_count, pairs):
    rows = pairs * LANES // group_count
    me, at = lax.axis_index("grp"), lax.axis_index("grp")
    bits = group_count.bit_length() - 1
    for k in range(1, bits):
        at = at + (1 - 2 * ((me // (1 << k)) % 2)) * (1 << k)
    span = 2 * rows if bits else rows
    return at // 2 * span // LANES, min(pairs, -(-span // LANES) + 1)


class WeightGather:
    def __init__(self, group_count, shard, full, send, far, near):
        self.shard, self.full = shard, full
        self.send, self.far_sem, self.near_sem = send, far, near
        self.rows = shard.shape[0]
        self.unit = 16 if self.rows % 16 == 0 else 8
        self.bits = group_count.bit_length() - 1
        self.far = list(range(1, self.bits))
        self.parts = row_parts(self.rows, max(1, len(self.far)), self.unit)
        self.me = lax.axis_index("grp")

    def flip(self, mask):
        at = self.me
        for k in range(self.bits):
            if mask >> k & 1:
                at = at + (1 - 2 * ((self.me // (1 << k)) % 2)) * (1 << k)
        return at

    def order(self, j):
        return self.far[j:] + self.far[:j] if self.far else []

    def masks(self, level):
        return [m for m in range(0, 1 << self.bits, 2) if bin(m).count("1") == level]

    def cuts(self, j, mask):
        first, size = self.parts[j]
        if mask.bit_count() < len(self.far):
            return [(first, size)]
        head = size * 2 // 3 // self.unit * self.unit
        return [(first, head), (first + head, size - head)]

    def piece(self, mask, rows):
        return self.full.at[pl.ds(pl.multiple_of(self.flip(mask) * self.rows + rows[0], self.unit), rows[1]), :]

    def source(self, mask, rows):
        return self.shard.at[pl.ds(*rows), :] if mask == 0 else self.piece(mask, rows)

    def shards(self, count):
        return self.full.at[pl.ds(0, count * self.rows), :]

    def own(self):
        return pltpu.make_async_copy(
            self.shard, self.full.at[pl.ds(pl.multiple_of(self.me * self.rows, self.unit), self.rows), :],
            self.near_sem.at[0])

    def wait(self, count, sem):
        pltpu.make_async_copy(self.shards(count), self.shards(count), sem).wait()

    def near(self, mask, rows):
        if self.bits:
            remote(self.source(mask, rows), self.piece(mask, rows), self.send, self.near_sem.at[mask.bit_count()],
                   "grp", self.flip(1)).start()

    def advance(self, level):
        if level > 0:
            self.wait(len(self.masks(level)), self.far_sem.at[level])
        for mask in self.masks(level):
            for j in range(len(self.parts)):
                order = self.order(j)
                done = max([order.index(k) for k in order if mask >> k & 1], default=-1)
                for k in order[done + 1:]:
                    there = mask | 1 << k
                    for i, rows in enumerate(self.cuts(j, there)):
                        remote(self.source(mask, rows), self.piece(mask, rows), self.send,
                               self.far_sem.at[level + 1 + i], "grp", self.flip(1 << k)).start()
                self.near(mask, self.parts[j])
        if level == 0:
            self.own().start()

    def advance_last(self, i):
        level = len(self.far)
        if level == 0:
            return
        (mask,) = self.masks(level)
        ranges = [self.cuts(j, mask)[i] for j in range(len(self.parts))]
        ref = self.full.at[pl.ds(0, sum(size for _, size in ranges)), :]
        pltpu.make_async_copy(ref, ref, self.far_sem.at[level + i]).wait()
        for rows in ranges:
            self.near(mask, rows)

    def finish(self, level):
        if level <= len(self.far):
            self.wait((len(self.masks(level)) if self.bits else 0) + (level == 0), self.near_sem.at[level])

    def drain(self):
        far = 1 << len(self.far)
        if self.bits:
            self.wait(far - 1 + far, self.send)


def block_kernel(
    n, group_count, head_size,
    length_in, img, txt, image_shard, text_shard, gates_in,
    out_img, text_full, attended, text_acc, gates, length,
    qkv, shared_kv, shared_q, done, keys, first_values, second_values, valid, image_full, image_acc,
    in_send, in_recv, out_send, out_recv, kv_send, kv_recv, shared_local, w_send, w_far, w_near, small_local,
):
    me = lax.axis_index("blk")
    image_rows, text_rows, width = img.shape[1], txt.shape[1], img.shape[2]
    span = image_rows + text_rows
    pairs = width // LANES
    base, extra = divmod(pairs, n)
    streams = ((img, 0, image_rows), (txt, image_rows, text_rows))

    weights = [
        WeightGather(group_count, shard, full, w_send.at[i], w_far.at[i], w_near.at[i])
        for i, (shard, full) in enumerate(((image_shard, image_full), (text_shard, text_full)))
    ]

    length_copy = pltpu.make_async_copy(length_in, length, small_local.at[0])
    gates_copy = pltpu.make_async_copy(gates_in, gates, small_local.at[1])

    barrier = pltpu.get_barrier_semaphore()
    for d in range(1, n):
        pl.semaphore_signal(barrier, inc=1, device_id={"blk": lax.rem(me + d, n)}, device_id_type=MESH)
    for k in range(weights[0].bits):
        pl.semaphore_signal(barrier, inc=1, device_id={"grp": weights[0].flip(1 << k)}, device_id_type=MESH)
    length_copy.start()
    gates_copy.start()
    pl.semaphore_wait(barrier, n - 1 + weights[0].bits)

    def columns(b, p):
        return pl.ds(pl.multiple_of((b * base + p) * LANES, LANES), LANES)

    def rows_of(b, first, count):
        return pl.ds(pl.multiple_of(b * span + first, 16), count)

    def in_copies(p, dest):
        return [
            remote(src.at[:, :, columns(dest, p)], qkv.at[p, :, rows_of(me, first, count), :],
                   in_send, in_recv.at[p], "blk", dest)
            for src, first, count in streams
        ]

    def own_copies(p):
        return [
            pltpu.make_async_copy(
                src.at[:, :, columns(me, p)], qkv.at[p, :, rows_of(me, first, count), :], in_recv.at[p])
            for src, first, count in streams
        ]

    middle = n // 2
    split = n % 2 == 0

    def out_copy(p, dest):
        across = jnp.where((me < middle) == (dest < middle), 0, 1) if split else 0
        return remote(done.at[p, dest], attended.at[me * base + p], out_send, out_recv.at[p, across], "blk", dest)

    def own_out(p):
        return pltpu.make_async_copy(done.at[p, me], attended.at[me * base + p], out_recv.at[p, 0])

    def wait_bytes(ref, sem):
        pltpu.make_async_copy(ref, ref, sem).wait()

    shared_cols = pl.ds(n * base * LANES, extra * LANES)

    halves = (range(middle), range(middle, n))
    doors = (middle - 1, middle)

    def kv_direct(dest, across):
        return [
            remote(src.at[pl.ds(1, 2), :, shared_cols], shared_kv.at[:, rows_of(me, first, count), :],
                   kv_send, kv_recv.at[across], "blk", dest)
            for src, first, count in streams
        ]

    def kv_onward(owner, dest):
        block = shared_kv.at[:, rows_of(owner, 0, span), :]
        return remote(block, block, kv_send, kv_recv.at[1], "blk", dest)

    def kv_wait(blocks, sem):
        if blocks:
            wait_bytes(shared_kv.at[:, pl.ds(0, blocks * span), :], sem)

    def shared_own():
        copies = []
        for src, first, count in streams:
            copies.append(pltpu.make_async_copy(
                src.at[pl.ds(1, 2), :, shared_cols], shared_kv.at[:, rows_of(me, first, count), :], kv_recv.at[0]))
            copies.append(pltpu.make_async_copy(
                src.at[0, :, shared_cols], shared_q.at[pl.ds(first, count), :], shared_local))
        return copies

    def each_half(act):
        for side in range(2):
            if len(halves[side]):
                @pl.when((me < middle) if side == 0 else (me >= middle))
                def _():
                    act(side)

    def start_shared():
        def act(side):
            if len(halves[1 - side]):
                for copy in kv_direct(doors[1 - side], 1):
                    copy.start()
            for dest in halves[side]:
                @pl.when(dest != me)
                def _():
                    for copy in kv_direct(dest, 0):
                        copy.start()

        each_half(act)
        for copy in shared_own():
            copy.start()

    def pass_shared():
        def act(side):
            @pl.when(me == doors[side])
            def _():
                kv_wait(len(halves[1 - side]), kv_recv.at[1])
                for owner in halves[1 - side]:
                    for dest in halves[side]:
                        if dest != doors[side]:
                            kv_onward(owner, dest).start()

        each_half(act)

    def finish_shared():
        wait_bytes(shared_q, shared_local)

        def act(side):
            kv_wait(len(halves[side]), kv_recv.at[0])

            @pl.when(me != doors[side])
            def _():
                kv_wait(len(halves[1 - side]), kv_recv.at[1])

        each_half(act)

    def drain_shared():
        def act(side):
            own, other = len(halves[side]), len(halves[1 - side])
            kv_wait(own - 1 + (other > 0), kv_send)

            @pl.when(me == doors[side])
            def _():
                for _ in range(own - 1):
                    kv_wait(other, kv_send)

        each_half(act)

    order = sorted(range(1, n), key=lambda d: abs(d - n / 2))

    def send_in(p):
        for d in order:
            for copy in in_copies(p, lax.rem(me + d, n)):
                copy.start()
        for copy in own_copies(p):
            copy.start()

    first_half = lax.broadcasted_iota(jnp.int32, (span, LANES), 1) < head_size

    def prepare(block_keys, block_values):
        half = lax.broadcasted_iota(jnp.int32, (n * span, LANES), 1) < head_size
        ones = jnp.ones((n * span, LANES), jnp.bfloat16)
        usable = valid[...]
        k = block_keys()
        keys[...] = jnp.where(usable > 0.5, k, jnp.broadcast_to(k[0:1], k.shape))
        v = block_values()
        first_values[...] = jnp.where(half, v, ones) * usable
        second_values[...] = jnp.where(half, ones, v) * usable

    def attend_rows(queries):
        queries = queries * jnp.asarray(head_size ** (-0.5), jnp.bfloat16)
        zeros = jnp.zeros_like(queries)
        parts = []
        for own, values in ((jnp.where(first_half, queries, zeros), first_values),
                            (jnp.where(first_half, zeros, queries), second_values)):
            scores = lax.dot_general(own, keys[...], (((1,), (1,)), ((), ())), preferred_element_type=jnp.float32)
            probs = jnp.exp(scores - jnp.max(scores, axis=1, keepdims=True)).astype(jnp.bfloat16)
            parts.append(jnp.dot(probs, values[...], preferred_element_type=jnp.float32))
        summed = jnp.where(first_half, parts[0], parts[1])
        totals = pltpu.roll(jnp.where(first_half, parts[1], parts[0]), head_size, axis=1)
        return (summed / totals).astype(jnp.bfloat16)

    def attend_pair(p):
        wait_bytes(qkv.at[p], in_recv.at[p])
        prepare(lambda: qkv[p, 1], lambda: qkv[p, 2])

        def one_block(j, _):
            dest = lax.rem(me + n // 2 + j, n)
            done[p, dest] = attend_rows(qkv[p, 0, rows_of(dest, 0, span), :])

            @pl.when(dest != me)
            def _():
                out_copy(p, dest).start()

            return 0

        lax.fori_loop(0, n, one_block, 0)
        own_out(p).start()

    def attend_shared():
        finish_shared()
        for e in range(extra):
            cols = pl.ds(e * LANES, LANES)
            prepare(lambda: shared_kv[0, :, cols], lambda: shared_kv[1, :, cols])
            attended[n * base + e] = attend_rows(shared_q[:, cols])

    def project(acc, full, rows, chosen, start, finish):
        left = jnp.concatenate([attended[c, rows, :] for c in chosen], axis=1)
        for at, size in column_tiles(width, 256):
            right = jnp.concatenate([full[pl.ds(pl.multiple_of(c * LANES, LANES), LANES), pl.ds(at, size)] for c in chosen], axis=0)
            part = jnp.dot(left, right, preferred_element_type=jnp.float32)
            if not start:
                part = part + acc[:, pl.ds(at, size)]
            if finish is None:
                acc[:, pl.ds(at, size)] = part
            else:
                out, gate = finish
                out[:, pl.ds(at, size)] = (part * gates[0, pl.ds(gate, 1), pl.ds(at, size)]).astype(jnp.bfloat16)

    def text_step(c):
        part = jnp.dot(attended[c, text_span, :], text_full[pl.ds(pl.multiple_of(c * LANES, LANES), LANES), :],
                       preferred_element_type=jnp.float32)
        text_acc[...] += part

    def early_text(first, stride, count):
        def step(i, _):
            c = first + stride * i

            @pl.when(lax.rem(c - late_first + pairs, pairs) >= late_pairs)
            def _():
                text_step(c)

            return 0

        lax.fori_loop(0, count, step, 0)

    late_first, late_pairs = late_rows(group_count, pairs)

    text_span = pl.ds(image_rows, text_rows)
    image_span = pl.ds(0, image_rows)

    if extra:
        start_shared()
    send_in(0)
    weights[0].advance(0)
    for p in range(1, base):
        send_in(p)
    weights[1].advance(0)

    length_copy.wait()
    for b in range(n):
        at = lax.broadcasted_iota(jnp.int32, (span, LANES), 0)
        usable = (at >= image_rows) | (b * image_rows + at < length[0])
        valid[pl.ds(b * span, span), :] = jnp.where(usable, 1.0, 0.0).astype(jnp.bfloat16)

    far_levels = len(weights[0].far)

    def advance(i, level):
        if level < far_levels:
            weights[i].advance(level)

    if extra:
        pass_shared()
    for p in range(base):
        if p == base - 1:
            if extra:
                attend_shared()
            for level in range(1 if base == 1 else 2, far_levels):
                weights[0].advance(level)
            for i in range(2):
                weights[0].advance_last(i)
        attend_pair(p)
        if p == 0 and base > 1:
            advance(0, 1)
        if p == min(1, base - 1):
            advance(1, 1)
    for level in range(far_levels + 1):
        weights[0].finish(level)
    gates_copy.wait()

    def wait_out(p, across):
        wait_bytes(attended.at[pl.ds(0, n // 2 if split else n)], out_recv.at[p, across])

    for level in range(2, far_levels):
        weights[1].advance(level)
    for level in range(far_levels):
        weights[1].finish(level)
    text_acc[...] = jnp.zeros_like(text_acc)
    started = bool(extra)
    if extra:
        project(image_acc, image_full, image_span, [n * base + e for e in range(extra)], True, None)
        early_text(n * base, 1, extra)
    if base < 3:
        weights[1].advance_last(0)
    near_first = jnp.where(me < middle, 0, middle) if split else 0
    for p in range(base):
        last = p == base - 1
        if p >= base - 2 and split:
            groups = [(near_first, n // 2, 0), (middle - near_first, n // 2, 1)]
        else:
            groups = [(0, n, 0)]
        for first, count, across in groups:
            wait_out(p, across)
            if split and len(groups) == 1:
                wait_out(p, 1)
            if p == max(0, base - 2) and across == len(groups) - 1:
                weights[1].advance_last(1)
            ends = last and across == len(groups) - 1
            project(image_acc, image_full, image_span, [(first + b) * base + p for b in range(count)], not started,
                    (out_img, 0) if ends else None)
            started = True
            if not ends:
                early_text(first * base + p, base, count)
        if p == base - 3:
            weights[1].advance_last(0)
    weights[1].finish(far_levels)

    wait_bytes(qkv.at[:, :, pl.ds(0, (n - 1) * span), :], in_send)
    for _ in range(base):
        wait_bytes(attended.at[pl.ds(0, n - 1)], out_send)
    if extra:
        drain_shared()
    for weight in weights:
        weight.drain()


def store_kernel(n, group_count, image_in, text_full, attended, text_acc, gates, image_out, text_out, text_done, sems):
    image_copy = pltpu.make_async_copy(image_in, image_out, sems.at[0])
    image_copy.start()
    pairs, text_rows = attended.shape[0], text_done.shape[0]
    image_rows = attended.shape[1] - text_rows
    base = pairs // n
    late_first, late_pairs = late_rows(group_count, pairs)
    left, chosen = [], []
    for i in range(late_pairs):
        c = lax.rem(late_first + i, pairs)
        left.append(attended[c, pl.ds(image_rows, text_rows), :])
        chosen.append(c)
    middle, count = n // 2, n // 2 if n % 2 == 0 else n
    first = jnp.where(lax.axis_index("blk") < middle, middle, 0) if n % 2 == 0 else 0
    for b in range(count):
        c = (first + b) * base + base - 1
        rows = attended[c, pl.ds(image_rows, text_rows), :]
        left.append(jnp.where(lax.rem(c - late_first + pairs, pairs) >= late_pairs, rows, jnp.zeros_like(rows)))
        chosen.append(c)
    left = jnp.concatenate(left, axis=1)
    for at, size in column_tiles(text_done.shape[1], 256):
        cols = pl.ds(at, size)
        right = jnp.concatenate(
            [text_full[pl.ds(pl.multiple_of(c * LANES, LANES), LANES), cols] for c in chosen], axis=0)
        total = text_acc[:, cols] + jnp.dot(left, right, preferred_element_type=jnp.float32)
        text_done[:, cols] = (total * gates[0, 1:2, cols]).astype(jnp.bfloat16)
    text_copy = pltpu.make_async_copy(text_done, text_out, sems.at[1])
    text_copy.start()
    text_copy.wait()
    image_copy.wait()


def store(n, group_count, outs):
    image, text_full, attended, text_acc, gates = [pltpu.with_memory_space_constraint(x, pltpu.VMEM) for x in outs]
    text = jax.ShapeDtypeStruct(text_acc.shape, jnp.bfloat16)
    vmem, hbm = pl.BlockSpec(memory_space=pltpu.VMEM), pl.BlockSpec(memory_space=pltpu.HBM)
    return pl.pallas_call(
        functools.partial(store_kernel, n, group_count),
        out_shape=(jax.ShapeDtypeStruct(image.shape, image.dtype), text),
        in_specs=[vmem] * 5,
        out_specs=(hbm, hbm),
        scratch_shapes=[
            pltpu.VMEM(text.shape, text.dtype), pltpu.SemaphoreType.DMA((2,)),
        ],
        compiler_params=pltpu.CompilerParams(vmem_limit_bytes=8 * 1024 * 1024),
        name="store",
    )(image, text_full, attended, text_acc, gates)


def per_device(image_tokens, text_tokens, lengths, image_weight, text_weight, gate_values):
    image_rows, text_rows, width = image_tokens.shape[1], text_tokens.shape[1], image_tokens.shape[2]
    n, group_count = lax.axis_size("blk"), lax.axis_size("grp")
    span = image_rows + text_rows
    pairs = width // LANES
    base, extra = divmod(pairs, n)
    bits = group_count.bit_length() - 1
    levels = max(1, bits)
    dma = pltpu.SemaphoreType.DMA
    bf16, f32 = jnp.bfloat16, jnp.float32
    any_space = pl.BlockSpec(memory_space=pltpu.HBM)
    vmem = pl.BlockSpec(memory_space=pltpu.VMEM)
    wide = max(1, extra) * LANES
    outs = pl.pallas_call(
        functools.partial(block_kernel, n, group_count, width // HEADS),
        out_shape=(
            pltpu.VMEM((image_rows, width), bf16),
            pltpu.VMEM((width, width), bf16),
            pltpu.VMEM((pairs, span, LANES), bf16),
            pltpu.VMEM((text_rows, width), f32),
            pltpu.VMEM((1, 2, width), f32),
        ),
        in_specs=[any_space] * 6,
        out_specs=(vmem,) * 5,
        scratch_shapes=[
            pltpu.SMEM((1,), jnp.int32),
            pltpu.VMEM((base, 3, n * span, LANES), bf16),
            pltpu.VMEM((2, n * span, wide), bf16),
            pltpu.VMEM((span, wide), bf16),
            pltpu.VMEM((base, n, span, LANES), bf16),
            pltpu.VMEM((n * span, LANES), bf16),
            pltpu.VMEM((n * span, LANES), bf16),
            pltpu.VMEM((n * span, LANES), bf16),
            pltpu.VMEM((n * span, LANES), bf16),
            pltpu.VMEM((width, width), bf16),
            pltpu.VMEM((image_rows, width), f32),
            dma, dma((base,)), dma, dma((base, 2)), dma, dma((2,)), dma,
            dma((2,)), dma((2, levels + 1)), dma((2, levels)), dma((2,)),
        ],
        compiler_params=pltpu.CompilerParams(
            collective_id=0, has_side_effects=True, vmem_limit_bytes=47 * 1024 * 1024
        ),
        name="attend",
    )(lengths, image_tokens, text_tokens, image_weight, text_weight, gate_values)
    return store(n, group_count, outs)


def solution(mesh):
    in_specs = (
        P(None, ("grp", "blk"), None),
        P(None, ("grp", "blk"), None),
        P("grp"),
        P("grp", None),
        P("grp", None),
        P("grp", None, None),
    )
    out_specs = (P(("grp", "blk"), None), P(("grp", "blk"), None))
    return jax.shard_map(
        per_device, mesh=mesh, in_specs=in_specs, out_specs=out_specs, check_vma=False
    )
```
